32 devices in a mesh: groups: 2 (over y), grid: 16 (over z, x, core).
Axes of the slice: x: 2, y: 2, z: 4, core: 2. Of those that a mesh axis runs over, the one named last changes fastest.
Arguments:
- start_field: float32 [32, 1024, 128], P(('groups', 'grid')), parts along dimension 0, may hold values from -6 to 6
- col_speed: float32 [1024], replicated, may hold values from 0.5 to 2
- row_speed: float32 [32], replicated, may hold values from 0.5 to 2
- levels: int32 [32], P('groups'), parts along dimension 0, may hold values from 2 to 5, as said below
- coeffs: int32 [32], P('groups'), parts along dimension 0, may hold values from 1 to 3
- assign_first: int32 [32], P('groups'), parts along dimension 0, may hold values from 0 to 15, each once
- assign_second: int32 [32], P('groups'), parts along dimension 0, may hold values from 0 to 15, each once
- owner_of: int32 [32], P('groups'), parts along dimension 0, may hold values from 0 to 15, each once
Outputs:
- combined: float32 [2048, 1280], P(('groups', 'grid')), parts along dimension 0
- final_field: float32 [32, 1024, 128], P(('groups', 'grid')), parts along dimension 0
The draws below stay inside these ranges and needn't reach their ends.
There are 2 independent parts, one for each index of `groups`. The reference program is written for one: setup_inputs(seed, part) draws one part's arguments, and reference() takes and returns one part's arrays. A program takes and returns all parts, laid end to end along the dimension named above; an argument that names none is the same for every part. Nothing has to cross between parts.
Inputs may be any that keep to these rules, and one draw needn't show every extreme that they name: `levels`: every run of 4 consecutive grids starting at a multiple of 4 holds each first level from 2 to 5 exactly once.
All inputs are finite; a program needn't handle non-finite values.
Results may differ from the reference program's by a relative error of at most 0.0003.
Values sent between devices are 32-bit elements; how exact they have to be, the bound alone decides.
A program may use at most 64 MiB of HBM per device.

```python
import math
import jax
import jax.numpy as jnp
import numpy as np
from jax import lax

LMIN = 2
NLEV = 4
CLEV = 5
STEPS = 2
ROWS = 128
COLS = 1024
CROWS = 320
FINE = 32
NGRID = 16
NPOS = 4
BLOCK_COLS = 64
N_GRID = 16


def draw_levels(key, part):
    rows_of = NGRID // NLEV
    scores = jax.random.randint(key, (rows_of, NLEV), 0, 1 << 20)
    scores = scores * NLEV + jnp.arange(NLEV, dtype=jnp.int32)[None, :]
    order_of = jnp.argsort(scores, axis=1)
    return (LMIN + order_of).reshape(NGRID).astype(jnp.int32)


def with_ends(drawn, rng, least, high):
    shape = drawn.shape
    index_at = [jax.random.randint(jax.random.fold_in(rng, axis), (), 0, shape[axis]) for axis in range(len(shape))]
    drawn = drawn.at[tuple(index_at)].set(least)
    longest = shape.index(max(shape))
    index_at[longest] = (index_at[longest] + 1) % shape[longest]
    return drawn.at[tuple(index_at)].set(high)


def steps_of(stream_key, dims, pieces, low, top_value):
    def one(axis_at, parts):
        draws = jax.random.uniform(jax.random.fold_in(jax.random.fold_in(stream_key, 6), axis_at), (parts,), jnp.float32, low / len(pieces), top_value / len(pieces))
        return jnp.repeat(jnp.exp(draws), dims[axis_at] // parts).reshape((-1,) + (1,) * (len(dims) - axis_at - 1))

    level = one(*pieces[0])
    for cut in pieces[1:]:
        level = level * one(*cut)
    return level


def normal_values(stream_key, extent, deviation, most, pieces=(), held_as=jnp.bfloat16):
    drawn = jax.random.normal(stream_key, extent, jnp.float32) * deviation
    if len(pieces) > 0:
        drawn = steps_of(stream_key, extent, pieces, -0.22, 0.18) * drawn
    return jnp.clip(drawn, min=-most, max=most).astype(held_as)


def setup_inputs(seed: int = 0, part: int = 0) -> dict:
    keys = jax.random.split(jax.random.key(seed), 9)
    own_keys = jax.random.split(jax.random.fold_in(keys[8], part), 9)
    start_field = normal_values(own_keys[0], (N_GRID, COLS, ROWS), 1.0, 6.0, ((0, 16),), jnp.float32)
    col_speed = jnp.clip(jnp.exp(jax.random.uniform(keys[1], (COLS,), jnp.float32, math.log(0.5), math.log(2.0))), 0.5, 2.0)
    row_speed = jnp.clip(jnp.exp(jax.random.uniform(keys[2], (FINE,), jnp.float32, math.log(0.5), math.log(2.0))), 0.5, 2.0)
    levels = draw_levels(jax.random.fold_in(jax.random.fold_in(keys[8], part), 71), part)
    coeffs = with_ends(jax.random.randint(own_keys[4], (NGRID,), 1, 4), jax.random.fold_in(own_keys[4], 1), 1, 3).astype(jnp.int32)
    assign_first = jax.random.permutation(own_keys[5], NGRID).astype(jnp.int32)
    assign_second = jax.random.permutation(own_keys[6], NGRID).astype(jnp.int32)
    owner_of = jax.random.permutation(own_keys[7], N_GRID).astype(jnp.int32)
    return {"start_field": start_field, "col_speed": col_speed, "row_speed": row_speed, "levels": levels, "coeffs": coeffs, "assign_first": assign_first, "assign_second": assign_second, "owner_of": owner_of}


time_step = 0.02
diffusivity = 0.0024
highest = lax.Precision.HIGHEST


def hier_line(line_level):
    points = 2 ** line_level
    matrix = np.zeros((points, points))
    matrix[0, 0] = 1.0
    for tier_rank in range(1, line_level + 1):
        stride = 2 ** (line_level - tier_rank)
        for entry_at in range(2 ** (tier_rank - 1), 2 ** tier_rank):
            node_at = (2 * (entry_at - 2 ** (tier_rank - 1)) + 1) * stride
            matrix[entry_at, node_at] += 1.0
            matrix[entry_at, (node_at - stride) % points] -= 0.5
            matrix[entry_at, (node_at + stride) % points] -= 0.5
    return matrix


def dehier_line(line_level):
    points = 2 ** line_level
    matrix = np.zeros((points, points))
    matrix[0, 0] = 1.0
    for tier_rank in range(1, line_level + 1):
        stride = 2 ** (line_level - tier_rank)
        for entry_at in range(2 ** (tier_rank - 1), 2 ** tier_rank):
            node_at = (2 * (entry_at - 2 ** (tier_rank - 1)) + 1) * stride
            matrix[node_at] = 0.5 * (matrix[(node_at - stride) % points] + matrix[(node_at + stride) % points])
            matrix[node_at, entry_at] += 1.0
    return matrix


def row_tables():
    row_bits = 2 * LMIN + NLEV - 1
    starts, widths, offsets = [], [], []
    running = 0
    for piece_level in range(LMIN, LMIN + NLEV):
        first_row = 0 if piece_level == LMIN else 2 ** (piece_level - 1)
        breadth = 2 ** LMIN if piece_level == LMIN else 2 ** (piece_level - 1)
        starts.append(first_row)
        widths.append(breadth)
        offsets.append(running)
        running += breadth * 2 ** (row_bits - piece_level)
    forward, backward, embeds, places = [], [], [], []
    for shift_level in range(NLEV):
        first_level = LMIN + shift_level
        second_level = row_bits - first_level
        tensor = np.kron(hier_line(first_level), hier_line(second_level))
        inverse = np.kron(dehier_line(first_level), dehier_line(second_level))
        order_list, place_list = [], []
        for slot_index in range(shift_level + 1):
            for second in range(2 ** second_level):
                for first_idx in range(starts[slot_index], starts[slot_index] + widths[slot_index]):
                    order_list.append(first_idx * 2 ** second_level + second)
                    place_list.append(offsets[slot_index] + second * widths[slot_index] + first_idx - starts[slot_index])
        embedding = np.zeros((running, 2 ** row_bits))
        embedding[np.array(place_list), np.arange(2 ** row_bits)] = 1.0
        forward.append(tensor[order_list])
        backward.append(inverse[:, order_list])
        embeds.append(embedding)
        places.append(place_list)
    return (jnp.asarray(np.stack(forward), jnp.float32), jnp.asarray(np.stack(backward), jnp.float32),
            jnp.asarray(np.stack(embeds), jnp.float32), jnp.asarray(np.array(places), jnp.int32))


def column_pass(values, matrix):
    side_cells = matrix.shape[0]
    cube_view = values.reshape(side_cells, side_cells, values.shape[-1])
    cube_view = jnp.einsum('ab,bjr->ajr', matrix, cube_view, precision=highest)
    cube_view = jnp.einsum('ab,jbr->jar', matrix, cube_view, precision=highest)
    return cube_view.reshape(values.shape)


def advance(values, grid_level, count, col_speed, row_speed):
    side_cells = 2 ** CLEV
    total_rows = values.shape[1]
    row_bits = 2 * LMIN + NLEV - 1
    other_level = row_bits - grid_level
    inner_count = jnp.left_shift(jnp.int32(1), other_level)
    inner_pos = jnp.bitwise_and(jnp.arange(total_rows, dtype=jnp.int32), inner_count - 1)
    sample_at = inner_pos * jnp.left_shift(jnp.int32(1), row_bits - LMIN - other_level)
    fine_cells = row_speed.shape[0]
    row_factor = jnp.sum(jnp.where(sample_at[:, None] == jnp.arange(fine_cells, dtype=jnp.int32)[None, :],
                                   row_speed[None, :], jnp.zeros_like(row_speed)[None, :]), axis=1)
    velocity = col_speed[:, None] * row_factor[None, :]
    refine = jnp.left_shift(jnp.int32(1), grid_level - LMIN)
    dt_sub = time_step / refine.astype(jnp.float32)
    scale_one = jnp.left_shift(jnp.int32(1), grid_level).astype(jnp.float32)
    scale_two = inner_count.astype(jnp.float32)
    coeff_side = float(4 ** CLEV)
    at_last = (inner_pos == inner_count - 1)[None, :]
    at_first = (inner_pos == 0)[None, :]

    def one_substep(turn_index, current):
        up_one = jnp.roll(current, -inner_count, axis=1)
        down_one = jnp.roll(current, inner_count, axis=1)
        up_two = jnp.where(at_last, jnp.roll(current, inner_count - 1, axis=1), jnp.roll(current, -1, axis=1))
        down_two = jnp.where(at_first, jnp.roll(current, 1 - inner_count, axis=1), jnp.roll(current, 1, axis=1))
        cube_view = current.reshape(side_cells, side_cells, total_rows)
        across = (jnp.roll(cube_view, 1, axis=0) + jnp.roll(cube_view, -1, axis=0)
                  + jnp.roll(cube_view, 1, axis=1) + jnp.roll(cube_view, -1, axis=1))
        across = across.reshape(current.shape) - 4.0 * current
        spread = (scale_one * scale_one * (up_one + down_one - 2.0 * current)
                  + scale_two * scale_two * (up_two + down_two - 2.0 * current) + coeff_side * across)
        transport = velocity * (up_one - down_one) * (0.5 * scale_one)
        return current + dt_sub * (diffusivity * spread - transport)

    return lax.fori_loop(jnp.int32(0), refine * count, one_substep, values)


def reference(start_field, col_speed, row_speed, levels, coeffs, assign_first, assign_second, owner_of):
    forward, backward, embeds, places = row_tables()
    column_hier = jnp.asarray(hier_line(CLEV), jnp.float32)
    column_back = jnp.asarray(dehier_line(CLEV), jnp.float32)
    cover = jnp.sum(embeds, axis=2)
    grid_ids = jnp.arange(NGRID, dtype=jnp.int32)
    weights = coeffs.astype(jnp.float32)
    denominator = (weights[:, None] * cover[levels - LMIN]).reshape(NPOS, NLEV, CROWS).sum(axis=1)

    def hier_one(inputs):
        values, grid_level = inputs
        mixed = column_pass(values, column_hier)
        return jnp.dot(mixed, forward[grid_level - LMIN].T, precision=highest)

    def dehier_one(values, grid_level):
        mixed = jnp.dot(values, backward[grid_level - LMIN].T, precision=highest)
        return column_pass(mixed, column_back)

    def combine(surplus):
        def spread_one(inputs):
            values, grid_level, weight = inputs
            return jnp.dot(values * weight, embeds[grid_level - LMIN].T, precision=highest)
        placed = lax.map(spread_one, (surplus, levels, weights))
        total = placed.reshape(NPOS, NLEV, COLS, CROWS).sum(axis=1)
        return total / denominator[:, None, :]

    def restrict(section_values):
        def take_one(inputs):
            grid_id, grid_level = inputs
            return jnp.dot(section_values[grid_id // NLEV], embeds[grid_level - LMIN], precision=highest)
        return lax.map(take_one, (grid_ids, levels))

    def first_cycle(inputs):
        values, grid_level = inputs
        return advance(values, grid_level, STEPS, col_speed, row_speed)

    def later_cycle(inputs):
        values, grid_level = inputs
        return advance(dehier_one(values, grid_level), grid_level, STEPS, col_speed, row_speed)

    def last_step(inputs):
        values, grid_level = inputs
        return advance(dehier_one(values, grid_level), grid_level, 1, col_speed, row_speed)

    current = lax.map(first_cycle, (start_field[assign_first], levels))
    first_combined = combine(lax.map(hier_one, (current, levels)))
    current = lax.map(later_cycle, (restrict(first_combined), levels))
    second_combined = combine(lax.map(hier_one, (current, levels)))
    current = lax.map(last_step, (restrict(second_combined), levels))
    final_field = jnp.zeros_like(current).at[assign_second].set(current)
    owner_ids = jnp.arange(N_GRID, dtype=jnp.int32)
    owner_inv = jnp.sum(jnp.where(owner_of[None, :] == owner_ids[:, None], owner_ids[None, :], 0), axis=1)
    blocks = jnp.transpose(second_combined, (1, 0, 2)).reshape(N_GRID, BLOCK_COLS, NPOS * CROWS)
    combined = blocks[owner_inv].reshape(COLS, NPOS * CROWS)
    return combined, final_field
```

```python
import functools

import jax
import jax.numpy as jnp
import numpy as np
from jax import lax
from jax.experimental import pallas as pl
from jax.experimental.pallas import tpu as pltpu
from jax.sharding import PartitionSpec as P

LMIN = 2
NLEV = 4
CLEV = 5
STEPS = 2
SIDE = 2**CLEV
ROW_BITS = 2 * LMIN + NLEV - 1
LANES = 2**ROW_BITS

time_step = 0.02
diffusivity = 0.0024
MESH = pl.DeviceIdType.MESH
VMEM_SPEC = pl.BlockSpec(memory_space=pltpu.VMEM)
SMEM_SPEC = pl.BlockSpec(memory_space=pltpu.SMEM)


def hier_line(line_level):
    points = 2**line_level
    matrix = np.zeros((points, points))
    matrix[0, 0] = 1.0
    for tier_rank in range(1, line_level + 1):
        stride = 2 ** (line_level - tier_rank)
        for entry_at in range(2 ** (tier_rank - 1), 2**tier_rank):
            node_at = (2 * (entry_at - 2 ** (tier_rank - 1)) + 1) * stride
            matrix[entry_at, node_at] += 1.0
            matrix[entry_at, (node_at - stride) % points] -= 0.5
            matrix[entry_at, (node_at + stride) % points] -= 0.5
    return matrix


def dehier_line(line_level):
    points = 2**line_level
    matrix = np.zeros((points, points))
    matrix[0, 0] = 1.0
    for tier_rank in range(1, line_level + 1):
        stride = 2 ** (line_level - tier_rank)
        for entry_at in range(2 ** (tier_rank - 1), 2**tier_rank):
            node_at = (2 * (entry_at - 2 ** (tier_rank - 1)) + 1) * stride
            matrix[node_at] = 0.5 * (
                matrix[(node_at - stride) % points] + matrix[(node_at + stride) % points]
            )
            matrix[node_at, entry_at] += 1.0
    return matrix


def row_tables():
    starts, widths, offsets = ([], [], [])
    running = 0
    for piece_level in range(LMIN, LMIN + NLEV):
        first_row = 0 if piece_level == LMIN else 2 ** (piece_level - 1)
        breadth = 2**LMIN if piece_level == LMIN else 2 ** (piece_level - 1)
        starts.append(first_row)
        widths.append(breadth)
        offsets.append(running)
        running += breadth * 2 ** (ROW_BITS - piece_level)
    padded = -(-running // 128) * 128
    forward, backward, embeds = ([], [], [])
    for shift_level in range(NLEV):
        first_level = LMIN + shift_level
        second_level = ROW_BITS - first_level
        tensor = np.kron(hier_line(first_level), hier_line(second_level))
        inverse = np.kron(dehier_line(first_level), dehier_line(second_level))
        order_list, place_list = ([], [])
        for slot_index in range(shift_level + 1):
            for second in range(2**second_level):
                for first_idx in range(starts[slot_index], starts[slot_index] + widths[slot_index]):
                    order_list.append(first_idx * 2**second_level + second)
                    place_list.append(
                        offsets[slot_index]
                        + second * widths[slot_index]
                        + first_idx
                        - starts[slot_index]
                    )
        embedding = np.zeros((padded, LANES))
        embedding[np.array(place_list), np.arange(LANES)] = 1.0
        forward.append(tensor[order_list].T)
        backward.append(inverse[:, order_list].T)
        embeds.append(embedding)
    stacked = np.concatenate([e.T for e in embeds], axis=0)
    cover = np.stack([e.sum(axis=1) for e in embeds])
    return np.stack(forward), np.stack(backward), stacked, cover, running, padded


def tiers():
    found = []
    for tier_rank in range(1, CLEV + 1):
        stride = 2 ** (CLEV - tier_rank)
        for entry_at in range(2 ** (tier_rank - 1), 2**tier_rank):
            node_at = (2 * (entry_at - 2 ** (tier_rank - 1)) + 1) * stride
            found.append((entry_at, node_at, node_at - stride, (node_at + stride) % SIDE))
    return found


def split_dot(values, matrix):
    high = values.astype(jnp.bfloat16)
    low = (values - high.astype(jnp.float32)).astype(jnp.bfloat16)
    return jnp.dot(high, matrix, preferred_element_type=jnp.float32) + jnp.dot(
        low, matrix, preferred_element_type=jnp.float32
    )


def hier_lines(read, write):
    vals = [read(i) for i in range(SIDE)]
    write(0, vals[0])
    for entry_at, node_at, low_at, high_at in tiers():
        write(entry_at, vals[node_at] - 0.5 * (vals[low_at] + vals[high_at]))


def dehier_lines(read, write):
    vals = [None] * SIDE
    vals[0] = read(0)
    write(0, vals[0])
    for entry_at, node_at, low_at, high_at in tiers():
        vals[node_at] = read(entry_at) + 0.5 * (vals[low_at] + vals[high_at])
        write(node_at, vals[node_at])


def lines_first(op, buf, src, dst):
    for part in range(SIDE // 8):
        op(
            lambda i: buf[pl.ds(src + i * SIDE + part * 8, 8), :],
            lambda i, v: buf.__setitem__((pl.ds(dst + i * SIDE + part * 8, 8), slice(None)), v),
        )


def lines_second(op, buf, src, dst):
    for part in range(SIDE // 8):
        op(
            lambda i: buf[pl.ds(src + part * 8 * SIDE + i, 8, stride=SIDE), :],
            lambda i, v: buf.__setitem__(
                (pl.ds(dst + part * 8 * SIDE + i, 8, stride=SIDE), slice(None)), v
            ),
        )


def local_kernel(
    count, pre, post, in_map, out_map, tables, devices,
    levels, coeffs, assign, assign_next, owner, row_speed, x_ref, col_ref, *rest,
):
    rest = list(rest)
    back_ref = rest.pop(0) if pre else None
    fwd_ref = rest.pop(0) if post else None
    out_ref = rest.pop(0)
    tab_ref = rest.pop(0) if tables else None
    buf, plus, minus = rest
    cells = SIDE * SIDE
    block = cells // devices
    sections = devices // NLEV
    me = lax.axis_index("grid")

    if tables:
        def fill(g, carry):
            slot = (levels[g] - LMIN) * sections + g // NLEV
            tab_ref[slot] = assign[g]
            tab_ref[devices + slot] = assign_next[g]
            tab_ref[2 * devices + assign_next[g]] = slot
            tab_ref[3 * devices + slot] = coeffs[g]
            return carry
        lax.fori_loop(0, devices, fill, 0)

    own = lax.fori_loop(
        0, devices, lambda g, seen: jnp.where(assign[g] == me, g, seen), jnp.int32(0)
    )
    level = levels[own]
    inner = jnp.left_shift(jnp.int32(1), ROW_BITS - level)
    refine = jnp.left_shift(jnp.int32(1), level - LMIN)
    scale_one = jnp.left_shift(jnp.int32(1), level).astype(jnp.float32)
    scale_two = inner.astype(jnp.float32)
    dt = jnp.float32(time_step)
    for shift in range(1, NLEV):
        dt = jnp.where(level == LMIN + shift, jnp.float32(time_step / 2**shift), dt)
    k1 = dt * diffusivity * scale_one * scale_one
    k2 = dt * diffusivity * scale_two * scale_two
    k3 = dt * diffusivity * float(4**CLEV)
    k0 = 1.0 - 2.0 * k1 - 2.0 * k2 - 4.0 * k3

    lane = lax.broadcasted_iota(jnp.int32, (8, LANES), 1)
    inner_pos = jnp.bitwise_and(lane, inner - 1)
    sample_at = inner_pos * jnp.left_shift(jnp.int32(1), level - LMIN)
    row_factor = jnp.zeros((8, LANES), jnp.float32)
    for f in range(row_speed.shape[0]):
        row_factor = jnp.where(sample_at == f, row_speed[f], row_factor)
    row_factor = row_factor * (dt * 0.5 * scale_one)

    def speeds(i, carry):
        at = pl.multiple_of(i * 32, 32)
        vel = col_ref[pl.ds(at, 32), :] * jnp.concatenate([row_factor] * 4, axis=0)
        plus[pl.ds(at, 32), :] = k1 - vel
        minus[pl.ds(at, 32), :] = k1 + vel
        return carry
    lax.fori_loop(0, cells // 32, speeds, 0)

    if pre:
        def take(b, carry):
            buf[pl.ds(pl.multiple_of(b * block, block), block), :] = x_ref[owner[b] if in_map else b]
            return carry
        lax.fori_loop(0, devices, take, 0)
        weights = back_ref[level - LMIN]
        for at in range(0, cells, 256):
            buf[pl.ds(cells + at, 256), :] = split_dot(buf[pl.ds(at, 256), :], weights)
        lines_first(dehier_lines, buf, cells, 0)
        lines_second(dehier_lines, buf, 0, cells)
        start = 1
    else:
        buf[pl.ds(0, cells), :] = x_ref[0]
        start = 0

    pos_slab = jnp.concatenate([inner_pos] * 4, axis=0)
    at_first = pos_slab == 0
    at_last = pos_slab == inner - 1
    group = 4

    def substep(turn, parity):
        src = parity * cells
        dst = (1 - parity) * cells

        def slabs(i, carry):
            base = i * group
            cur = []
            for j in range(-1, group + 1):
                m = jnp.bitwise_and(base + j, SIDE - 1)
                cur.append(buf[pl.ds(pl.multiple_of(src + m * SIDE, SIDE), SIDE), :])
            for j in range(group):
                u = cur[j + 1]
                up1 = pltpu.roll(u, LANES - inner, 1)
                dn1 = pltpu.roll(u, inner, 1)
                up2 = pltpu.roll(jnp.where(at_first, dn1, u), LANES - 1, 1)
                dn2 = pltpu.roll(jnp.where(at_last, up1, u), 1, 1)
                side = (pltpu.roll(u, 1, 0) + pltpu.roll(u, SIDE - 1, 0)) + (cur[j] + cur[j + 2])
                at = pl.multiple_of((base + j) * SIDE, SIDE)
                new = k0 * u + plus[pl.ds(at, SIDE), :] * up1
                new = new + minus[pl.ds(at, SIDE), :] * dn1
                new = new + (k2 * (up2 + dn2) + k3 * side)
                buf[pl.ds(pl.multiple_of(dst + (base + j) * SIDE, SIDE), SIDE), :] = new
            return carry

        lax.fori_loop(0, SIDE // group, slabs, 0)
        return 1 - parity

    final = lax.fori_loop(0, refine * count, substep, jnp.int32(start))

    if post:
        src, dst = start * cells, (1 - start) * cells
        lines_first(hier_lines, buf, src, dst)
        lines_second(hier_lines, buf, dst, src)
        weight = coeffs[own].astype(jnp.float32)
        weights = fwd_ref[level - LMIN]
        for at in range(0, cells, 256):
            buf[pl.ds(dst + at, 256), :] = weight * split_dot(buf[pl.ds(src + at, 256), :], weights)

        def give(b, carry):
            out_ref[owner[b] if out_map else b] = buf[
                pl.ds(pl.multiple_of(dst + b * block, block), block), :
            ]
            return carry
        lax.fori_loop(0, devices, give, 0)
    else:
        out_ref[0] = buf[pl.ds(pl.multiple_of(final * cells, cells), cells), :]


def exchange_kernel(
    source_row, keep, devices, tab, x_ref, embed_ref, take_ref, cover_ref, out_ref, *rest
):
    rest = list(rest)
    keep_ref = rest.pop(0) if keep else None
    recv, wide, packs, send2, sems = rest
    block = x_ref.shape[1]
    sections = devices // NLEV
    padded = cover_ref.shape[1]
    me = lax.axis_index("grid")

    barrier = pltpu.get_barrier_semaphore()

    def greet(i, carry):
        pl.semaphore_signal(
            barrier, inc=1, device_id={"grid": lax.rem(me + i, devices)}, device_id_type=MESH
        )
        return carry

    lax.fori_loop(1, devices, greet, 0)
    pl.semaphore_wait(barrier, devices - 1)

    def copy_of(src, dst, base, i):
        to = lax.rem(me + i, devices)
        return pltpu.make_async_remote_copy(
            src_ref=src.at[to],
            dst_ref=dst.at[me],
            send_sem=sems.at[base, i],
            recv_sem=sems.at[base + 1, i],
            device_id={"grid": to},
            device_id_type=MESH,
        )

    def start_first(i, carry):
        copy_of(x_ref, recv, 0, i).start()
        return carry

    lax.fori_loop(1, devices, start_first, 0)
    recv[me] = x_ref[me]

    def wait_first(i, carry):
        copy_of(x_ref, recv, 0, i).wait()
        return carry

    lax.fori_loop(1, devices, wait_first, 0)

    def gather(q, carry):
        for lev in range(NLEV):
            wide[pl.ds(pl.multiple_of(q * block, block), block), lev * LANES : (lev + 1) * LANES] = recv[
                tab[source_row * devices + lev * sections + q]
            ]
        return carry

    lax.fori_loop(0, sections, gather, 0)
    total = split_dot(wide[...], embed_ref[...])
    wide[:, 0:padded] = total

    def divide(q, carry):
        denom = jnp.zeros((1, padded), jnp.float32)
        for lev in range(NLEV):
            denom = denom + cover_ref[lev : lev + 1, :] * tab[
                3 * devices + lev * sections + q
            ].astype(jnp.float32)
        inverse = 1.0 / jnp.where(denom > 0.0, denom, 1.0)
        at = pl.multiple_of(q * block, block)
        value = wide[pl.ds(at, block), 0:padded] * inverse
        wide[pl.ds(at, block), 0:padded] = value
        if keep:
            keep_ref[q] = value
        return carry

    lax.fori_loop(0, sections, divide, 0)
    picked = split_dot(wide[:, 0:padded], take_ref[...])
    for lev in range(NLEV):
        packs[pl.ds(lev * sections, sections)] = picked[:, lev * LANES : (lev + 1) * LANES].reshape(
            sections, block, LANES
        )

    def start_second(i, carry):
        to = lax.rem(me + i, devices)
        send2[to] = packs[tab[2 * devices + to]]
        copy_of(send2, out_ref, 2, i).start()
        return carry

    lax.fori_loop(1, devices, start_second, 0)
    out_ref[me] = packs[tab[2 * devices + me]]

    def wait_second(i, carry):
        copy_of(send2, out_ref, 2, i).wait()
        return carry

    lax.fori_loop(1, devices, wait_second, 0)


def local(start_field, col_speed, row_speed, levels, coeffs, assign_first, assign_second, owner_of):
    forward, backward, stacked, cover, section_rows, padded = row_tables()
    forward = jnp.asarray(forward, jnp.bfloat16)
    backward = jnp.asarray(backward, jnp.bfloat16)
    embed = jnp.asarray(stacked, jnp.bfloat16)
    take = jnp.asarray(stacked.T, jnp.bfloat16)
    cover = jnp.asarray(cover, jnp.float32)
    devices = lax.axis_size("grid")
    cells, lanes = start_field.shape[1:]
    block = cells // devices
    sections = devices // NLEV
    columns = jnp.broadcast_to(col_speed[:, None], (cells, lanes))

    def stage(x, assign, assign_next, count, pre, post, in_map, out_map, tables):
        args = [levels, coeffs, assign, assign_next, owner_of, row_speed, x, columns]
        specs = [SMEM_SPEC] * 6 + [VMEM_SPEC] * 2
        if pre:
            args.append(backward)
            specs.append(VMEM_SPEC)
        if post:
            args.append(forward)
            specs.append(VMEM_SPEC)
        shape = (devices, block, lanes) if post else (1, cells, lanes)
        outs = [jax.ShapeDtypeStruct(shape, jnp.float32)]
        out_specs = [VMEM_SPEC]
        if tables:
            outs.append(jax.ShapeDtypeStruct((4 * devices,), jnp.int32))
            out_specs.append(SMEM_SPEC)
        return pl.pallas_call(
            functools.partial(local_kernel, count, pre, post, in_map, out_map, tables, devices),
            out_shape=outs,
            in_specs=specs,
            out_specs=out_specs,
            scratch_shapes=[
                pltpu.VMEM((2 * cells, lanes), jnp.float32),
                pltpu.VMEM((cells, lanes), jnp.float32),
                pltpu.VMEM((cells, lanes), jnp.float32),
            ],
        )(*args)

    def exchange(x, tab, source_row, keep, collective_id):
        outs = [jax.ShapeDtypeStruct((devices, block, lanes), jnp.float32)]
        if keep:
            outs.append(jax.ShapeDtypeStruct((sections, block, padded), jnp.float32))
        return pl.pallas_call(
            functools.partial(exchange_kernel, source_row, keep, devices),
            out_shape=outs,
            in_specs=[SMEM_SPEC] + [VMEM_SPEC] * 4,
            out_specs=[VMEM_SPEC] * len(outs),
            scratch_shapes=[
                pltpu.VMEM((devices, block, lanes), jnp.float32),
                pltpu.VMEM((sections * block, NLEV * lanes), jnp.float32),
                pltpu.VMEM((devices, block, lanes), jnp.float32),
                pltpu.VMEM((devices, block, lanes), jnp.float32),
                pltpu.SemaphoreType.DMA((4, devices)),
            ],
            compiler_params=pltpu.CompilerParams(
                collective_id=collective_id, has_side_effects=True
            ),
        )(tab, x, embed, take, cover)

    outgoing, tab = stage(
        start_field, assign_first, assign_second, STEPS, False, True, False, False, True
    )
    (restricted,) = exchange(outgoing, tab, 0, False, 0)
    (outgoing,) = stage(
        restricted, assign_second, assign_second, STEPS, True, True, False, True, False
    )
    restricted, kept = exchange(outgoing, tab, 1, True, 1)
    (final,) = stage(restricted, assign_second, assign_second, 1, True, False, True, False, False)
    combined = jnp.transpose(kept[:, :, :section_rows], (1, 0, 2)).reshape(
        block, sections * section_rows
    )
    return combined, final


def solution(mesh):
    placed = (
        P(("groups", "grid"), None, None),
        P(),
        P(),
        P("groups"),
        P("groups"),
        P("groups"),
        P("groups"),
        P("groups"),
    )
    return jax.shard_map(
        local,
        mesh=mesh,
        in_specs=placed,
        out_specs=(P(("groups", "grid"), None), P(("groups", "grid"), None, None)),
        check_vma=False,
    )
```

```python
import functools

import jax
import jax.numpy as jnp
import numpy as np
from jax import lax
from jax.experimental import pallas as pl
from jax.experimental.pallas import tpu as pltpu
from jax.sharding import PartitionSpec as P

LMIN = 2
NLEV = 4
CLEV = 5
STEPS = 2
SIDE = 2**CLEV
ROW_BITS = 2 * LMIN + NLEV - 1
LANES = 2**ROW_BITS

time_step = 0.02
diffusivity = 0.0024
MESH = pl.DeviceIdType.MESH
VMEM_SPEC = pl.BlockSpec(memory_space=pltpu.VMEM)
SMEM_SPEC = pl.BlockSpec(memory_space=pltpu.SMEM)


def hier_line(line_level):
    points = 2**line_level
    matrix = np.zeros((points, points))
    matrix[0, 0] = 1.0
    for tier_rank in range(1, line_level + 1):
        stride = 2 ** (line_level - tier_rank)
        for entry_at in range(2 ** (tier_rank - 1), 2**tier_rank):
            node_at = (2 * (entry_at - 2 ** (tier_rank - 1)) + 1) * stride
            matrix[entry_at, node_at] += 1.0
            matrix[entry_at, (node_at - stride) % points] -= 0.5
            matrix[entry_at, (node_at + stride) % points] -= 0.5
    return matrix


def dehier_line(line_level):
    points = 2**line_level
    matrix = np.zeros((points, points))
    matrix[0, 0] = 1.0
    for tier_rank in range(1, line_level + 1):
        stride = 2 ** (line_level - tier_rank)
        for entry_at in range(2 ** (tier_rank - 1), 2**tier_rank):
            node_at = (2 * (entry_at - 2 ** (tier_rank - 1)) + 1) * stride
            matrix[node_at] = 0.5 * (
                matrix[(node_at - stride) % points] + matrix[(node_at + stride) % points]
            )
            matrix[node_at, entry_at] += 1.0
    return matrix


def row_tables():
    starts, widths, offsets = ([], [], [])
    running = 0
    for piece_level in range(LMIN, LMIN + NLEV):
        first_row = 0 if piece_level == LMIN else 2 ** (piece_level - 1)
        breadth = 2**LMIN if piece_level == LMIN else 2 ** (piece_level - 1)
        starts.append(first_row)
        widths.append(breadth)
        offsets.append(running)
        running += breadth * 2 ** (ROW_BITS - piece_level)
    padded = -(-running // 128) * 128
    forward, backward, embeds = ([], [], [])
    for shift_level in range(NLEV):
        first_level = LMIN + shift_level
        second_level = ROW_BITS - first_level
        tensor = np.kron(hier_line(first_level), hier_line(second_level))
        inverse = np.kron(dehier_line(first_level), dehier_line(second_level))
        order_list, place_list = ([], [])
        for slot_index in range(shift_level + 1):
            for second in range(2**second_level):
                for first_idx in range(starts[slot_index], starts[slot_index] + widths[slot_index]):
                    order_list.append(first_idx * 2**second_level + second)
                    place_list.append(
                        offsets[slot_index]
                        + second * widths[slot_index]
                        + first_idx
                        - starts[slot_index]
                    )
        embedding = np.zeros((padded, LANES))
        embedding[np.array(place_list), np.arange(LANES)] = 1.0
        forward.append(tensor[order_list].T)
        backward.append(inverse[:, order_list].T)
        embeds.append(embedding)
    stacked = np.concatenate([e.T for e in embeds], axis=0)
    cover = np.stack([e.sum(axis=1) for e in embeds])
    return np.stack(forward), np.stack(backward), stacked, cover, running, padded


def stencil_tables():
    tables = []
    for first_level in range(LMIN, LMIN + NLEV):
        inner = 2 ** (ROW_BITS - first_level)
        both = np.zeros((LANES, 2 * LANES))
        for row in range(LANES):
            base, pos = row - row % inner, row % inner
            both[row, row] -= 2.0 * (4**first_level + inner * inner)
            for sign in (1, -1):
                far = (row + sign * inner) % LANES
                near = base + (pos + sign) % inner
                both[far, row] += 4**first_level
                both[near, row] += inner * inner
                both[far, LANES + row] += sign
        tables.append(np.concatenate([both, both], axis=0))
    return np.stack(tables)


def tiers():
    found = []
    for tier_rank in range(1, CLEV + 1):
        stride = 2 ** (CLEV - tier_rank)
        for entry_at in range(2 ** (tier_rank - 1), 2**tier_rank):
            node_at = (2 * (entry_at - 2 ** (tier_rank - 1)) + 1) * stride
            found.append((entry_at, node_at, node_at - stride, (node_at + stride) % SIDE))
    return found


def split_dot(values, matrix):
    high = values.astype(jnp.bfloat16)
    low = (values - high.astype(jnp.float32)).astype(jnp.bfloat16)
    return jnp.dot(high, matrix, preferred_element_type=jnp.float32) + jnp.dot(
        low, matrix, preferred_element_type=jnp.float32
    )


def hier_lines(read, write):
    vals = [read(i) for i in range(SIDE)]
    write(0, vals[0])
    for entry_at, node_at, low_at, high_at in tiers():
        write(entry_at, vals[node_at] - 0.5 * (vals[low_at] + vals[high_at]))


def dehier_lines(read, write):
    vals = [None] * SIDE
    vals[0] = read(0)
    write(0, vals[0])
    for entry_at, node_at, low_at, high_at in tiers():
        vals[node_at] = read(entry_at) + 0.5 * (vals[low_at] + vals[high_at])
        write(node_at, vals[node_at])


def lines_first(op, buf, src, dst):
    for part in range(SIDE // 8):
        op(
            lambda i: buf[pl.ds(src + i * SIDE + part * 8, 8), :],
            lambda i, v: buf.__setitem__((pl.ds(dst + i * SIDE + part * 8, 8), slice(None)), v),
        )


def lines_second(op, buf, src, dst):
    for part in range(SIDE // 8):
        op(
            lambda i: buf[pl.ds(src + part * 8 * SIDE + i, 8, stride=SIDE), :],
            lambda i, v: buf.__setitem__(
                (pl.ds(dst + part * 8 * SIDE + i, 8, stride=SIDE), slice(None)), v
            ),
        )


def local_kernel(
    count, pre, post, in_map, out_map, tables, devices,
    levels, coeffs, assign, assign_next, owner, row_speed, x_ref, col_ref, stencil_ref, *rest,
):
    rest = list(rest)
    back_ref = rest.pop(0) if pre else None
    fwd_ref = rest.pop(0) if post else None
    out_ref = rest.pop(0)
    tab_ref = rest.pop(0) if tables else None
    buf, speed = rest
    cells = SIDE * SIDE
    block = cells // devices
    sections = devices // NLEV
    me = lax.axis_index("grid")

    if tables:
        def fill(g, carry):
            slot = (levels[g] - LMIN) * sections + g // NLEV
            tab_ref[slot] = assign[g]
            tab_ref[devices + slot] = assign_next[g]
            tab_ref[2 * devices + assign_next[g]] = slot
            tab_ref[3 * devices + slot] = coeffs[g]
            return carry
        lax.fori_loop(0, devices, fill, 0)

    own = lax.fori_loop(
        0, devices, lambda g, seen: jnp.where(assign[g] == me, g, seen), jnp.int32(0)
    )
    level = levels[own]
    inner = jnp.left_shift(jnp.int32(1), ROW_BITS - level)
    refine = jnp.left_shift(jnp.int32(1), level - LMIN)
    scale_one = jnp.left_shift(jnp.int32(1), level).astype(jnp.float32)
    dt = jnp.float32(time_step)
    for shift in range(1, NLEV):
        dt = jnp.where(level == LMIN + shift, jnp.float32(time_step / 2**shift), dt)
    k1 = dt * diffusivity
    k3 = dt * diffusivity * float(4**CLEV)
    k0 = 1.0 - 4.0 * k3

    lane = lax.broadcasted_iota(jnp.int32, (8, LANES), 1)
    inner_pos = jnp.bitwise_and(lane, inner - 1)
    sample_at = inner_pos * jnp.left_shift(jnp.int32(1), level - LMIN)
    row_factor = jnp.zeros((8, LANES), jnp.float32)
    for f in range(row_speed.shape[0]):
        row_factor = jnp.where(sample_at == f, row_speed[f], row_factor)
    row_factor = row_factor * (dt * 0.5 * scale_one)

    def speeds(i, carry):
        at = pl.multiple_of(i * 32, 32)
        speed[pl.ds(at, 32), :] = col_ref[pl.ds(at, 32), :] * jnp.concatenate([row_factor] * 4, axis=0)
        return carry
    lax.fori_loop(0, cells // 32, speeds, 0)

    if pre:
        def take(b, carry):
            buf[pl.ds(pl.multiple_of(b * block, block), block), :] = x_ref[owner[b] if in_map else b]
            return carry
        lax.fori_loop(0, devices, take, 0)
        weights = back_ref[level - LMIN]
        for at in range(0, cells, 256):
            buf[pl.ds(cells + at, 256), :] = split_dot(buf[pl.ds(at, 256), :], weights)
        lines_first(dehier_lines, buf, cells, 0)
        lines_second(dehier_lines, buf, 0, cells)
        start = 1
    else:
        buf[pl.ds(0, cells), :] = x_ref[0]
        start = 0

    group = 8
    rows = group * SIDE

    def substep(turn, parity):
        src = parity * cells
        dst = (1 - parity) * cells

        def slabs(i, carry):
            base = i * group
            at = pl.multiple_of(i * rows, rows)
            chunk = buf[pl.ds(pl.multiple_of(src + at, rows), rows), :]
            high = chunk.astype(jnp.bfloat16)
            low = (chunk - high.astype(jnp.float32)).astype(jnp.bfloat16)
            mixed = jnp.dot(
                jnp.concatenate([high, low], axis=1),
                stencil_ref[level - LMIN],
                preferred_element_type=jnp.float32,
            )
            cur = []
            for j in range(-1, group + 1):
                m = jnp.bitwise_and(base + j, SIDE - 1)
                cur.append(buf[pl.ds(pl.multiple_of(src + m * SIDE, SIDE), SIDE), :])
            for j in range(group):
                u = cur[j + 1]
                side = (pltpu.roll(u, 1, 0) + pltpu.roll(u, SIDE - 1, 0)) + (cur[j] + cur[j + 2])
                here = slice(j * SIDE, (j + 1) * SIDE)
                new = (k0 * u + k3 * side) + k1 * mixed[here, :LANES]
                new = new - speed[pl.ds(at + j * SIDE, SIDE), :] * mixed[here, LANES:]
                buf[pl.ds(pl.multiple_of(dst + (base + j) * SIDE, SIDE), SIDE), :] = new
            return carry

        lax.fori_loop(0, SIDE // group, slabs, 0)
        return 1 - parity

    final = lax.fori_loop(0, refine * count, substep, jnp.int32(start))

    if post:
        src, dst = start * cells, (1 - start) * cells
        lines_first(hier_lines, buf, src, dst)
        lines_second(hier_lines, buf, dst, src)
        weight = coeffs[own].astype(jnp.float32)
        weights = fwd_ref[level - LMIN]
        for at in range(0, cells, 256):
            buf[pl.ds(dst + at, 256), :] = weight * split_dot(buf[pl.ds(src + at, 256), :], weights)

        def give(b, carry):
            out_ref[owner[b] if out_map else b] = buf[
                pl.ds(pl.multiple_of(dst + b * block, block), block), :
            ]
            return carry
        lax.fori_loop(0, devices, give, 0)
    else:
        out_ref[0] = buf[pl.ds(pl.multiple_of(final * cells, cells), cells), :]


def exchange_kernel(
    source_row, keep, devices, tab, x_ref, embed_ref, take_ref, cover_ref, out_ref, *rest
):
    rest = list(rest)
    keep_ref = rest.pop(0) if keep else None
    recv, wide, packs, send2, sems = rest
    block = x_ref.shape[1]
    sections = devices // NLEV
    padded = cover_ref.shape[1]
    me = lax.axis_index("grid")

    barrier = pltpu.get_barrier_semaphore()

    def greet(i, carry):
        pl.semaphore_signal(
            barrier, inc=1, device_id={"grid": lax.rem(me + i, devices)}, device_id_type=MESH
        )
        return carry

    lax.fori_loop(1, devices, greet, 0)
    pl.semaphore_wait(barrier, devices - 1)

    def far_first(k):
        return lax.rem(k + devices // 2 - 1, devices - 1) + 1

    def copy_of(src, dst, base, i):
        to = lax.rem(me + i, devices)
        return pltpu.make_async_remote_copy(
            src_ref=src.at[to],
            dst_ref=dst.at[me],
            send_sem=sems.at[base, i],
            recv_sem=sems.at[base + 1, i],
            device_id={"grid": to},
            device_id_type=MESH,
        )

    def start_first(k, carry):
        i = far_first(k)
        copy_of(x_ref, recv, 0, i).start()
        return carry

    lax.fori_loop(0, devices - 1, start_first, 0)
    recv[me] = x_ref[me]

    def wait_first(i, carry):
        copy_of(x_ref, recv, 0, i).wait()
        return carry

    lax.fori_loop(1, devices, wait_first, 0)

    def gather(q, carry):
        for lev in range(NLEV):
            wide[pl.ds(pl.multiple_of(q * block, block), block), lev * LANES : (lev + 1) * LANES] = recv[
                tab[source_row * devices + lev * sections + q]
            ]
        return carry

    lax.fori_loop(0, sections, gather, 0)
    total = split_dot(wide[...], embed_ref[...])
    wide[:, 0:padded] = total

    def divide(q, carry):
        denom = jnp.zeros((1, padded), jnp.float32)
        for lev in range(NLEV):
            denom = denom + cover_ref[lev : lev + 1, :] * tab[
                3 * devices + lev * sections + q
            ].astype(jnp.float32)
        inverse = 1.0 / jnp.where(denom > 0.0, denom, 1.0)
        at = pl.multiple_of(q * block, block)
        value = wide[pl.ds(at, block), 0:padded] * inverse
        wide[pl.ds(at, block), 0:padded] = value
        if keep:
            keep_ref[q] = value
        return carry

    lax.fori_loop(0, sections, divide, 0)
    picked = split_dot(wide[:, 0:padded], take_ref[...])
    for lev in range(NLEV):
        packs[pl.ds(lev * sections, sections)] = picked[:, lev * LANES : (lev + 1) * LANES].reshape(
            sections, block, LANES
        )

    def start_second(k, carry):
        i = far_first(k)
        to = lax.rem(me + i, devices)
        send2[to] = packs[tab[2 * devices + to]]
        copy_of(send2, out_ref, 2, i).start()
        return carry

    lax.fori_loop(0, devices - 1, start_second, 0)
    out_ref[me] = packs[tab[2 * devices + me]]

    def wait_second(i, carry):
        copy_of(send2, out_ref, 2, i).wait()
        return carry

    lax.fori_loop(1, devices, wait_second, 0)


def local(start_field, col_speed, row_speed, levels, coeffs, assign_first, assign_second, owner_of):
    forward, backward, stacked, cover, section_rows, padded = row_tables()
    forward = jnp.asarray(forward, jnp.bfloat16)
    backward = jnp.asarray(backward, jnp.bfloat16)
    embed = jnp.asarray(stacked, jnp.bfloat16)
    take = jnp.asarray(stacked.T, jnp.bfloat16)
    cover = jnp.asarray(cover, jnp.float32)
    stencils = jnp.asarray(stencil_tables(), jnp.bfloat16)
    devices = lax.axis_size("grid")
    cells, lanes = start_field.shape[1:]
    block = cells // devices
    sections = devices // NLEV
    columns = jnp.broadcast_to(col_speed[:, None], (cells, lanes))

    def stage(x, assign, assign_next, count, pre, post, in_map, out_map, tables):
        args = [levels, coeffs, assign, assign_next, owner_of, row_speed, x, columns, stencils]
        specs = [SMEM_SPEC] * 6 + [VMEM_SPEC] * 3
        if pre:
            args.append(backward)
            specs.append(VMEM_SPEC)
        if post:
            args.append(forward)
            specs.append(VMEM_SPEC)
        shape = (devices, block, lanes) if post else (1, cells, lanes)
        outs = [jax.ShapeDtypeStruct(shape, jnp.float32)]
        out_specs = [VMEM_SPEC]
        if tables:
            outs.append(jax.ShapeDtypeStruct((4 * devices,), jnp.int32))
            out_specs.append(SMEM_SPEC)
        return pl.pallas_call(
            functools.partial(local_kernel, count, pre, post, in_map, out_map, tables, devices),
            out_shape=outs,
            in_specs=specs,
            out_specs=out_specs,
            scratch_shapes=[
                pltpu.VMEM((2 * cells, lanes), jnp.float32),
                pltpu.VMEM((cells, lanes), jnp.float32),
            ],
        )(*args)

    def exchange(x, tab, source_row, keep, collective_id):
        outs = [jax.ShapeDtypeStruct((devices, block, lanes), jnp.float32)]
        if keep:
            outs.append(jax.ShapeDtypeStruct((sections, block, padded), jnp.float32))
        return pl.pallas_call(
            functools.partial(exchange_kernel, source_row, keep, devices),
            out_shape=outs,
            in_specs=[SMEM_SPEC] + [VMEM_SPEC] * 4,
            out_specs=[VMEM_SPEC] * len(outs),
            scratch_shapes=[
                pltpu.VMEM((devices, block, lanes), jnp.float32),
                pltpu.VMEM((sections * block, NLEV * lanes), jnp.float32),
                pltpu.VMEM((devices, block, lanes), jnp.float32),
                pltpu.VMEM((devices, block, lanes), jnp.float32),
                pltpu.SemaphoreType.DMA((4, devices)),
            ],
            compiler_params=pltpu.CompilerParams(
                collective_id=collective_id, has_side_effects=True
            ),
        )(tab, x, embed, take, cover)

    outgoing, tab = stage(
        start_field, assign_first, assign_second, STEPS, False, True, False, False, True
    )
    (restricted,) = exchange(outgoing, tab, 0, False, 0)
    (outgoing,) = stage(
        restricted, assign_second, assign_second, STEPS, True, True, False, True, False
    )
    restricted, kept = exchange(outgoing, tab, 1, True, 1)
    (final,) = stage(restricted, assign_second, assign_second, 1, True, False, True, False, False)
    combined = jnp.transpose(kept[:, :, :section_rows], (1, 0, 2)).reshape(
        block, sections * section_rows
    )
    return combined, final


def solution(mesh):
    placed = (
        P(("groups", "grid"), None, None),
        P(),
        P(),
        P("groups"),
        P("groups"),
        P("groups"),
        P("groups"),
        P("groups"),
    )
    return jax.shard_map(
        local,
        mesh=mesh,
        in_specs=placed,
        out_specs=(P(("groups", "grid"), None), P(("groups", "grid"), None, None)),
        check_vma=False,
    )
```

```python
import functools

import jax
import jax.numpy as jnp
import numpy as np
from jax import lax
from jax.experimental import pallas as pl
from jax.experimental.pallas import tpu as pltpu
from jax.sharding import PartitionSpec as P

LMIN = 2
NLEV = 4
CLEV = 5
STEPS = 2
SIDE = 2**CLEV
ROW_BITS = 2 * LMIN + NLEV - 1
LANES = 2**ROW_BITS

time_step = 0.02
diffusivity = 0.0024
MESH = pl.DeviceIdType.MESH
VMEM_SPEC = pl.BlockSpec(memory_space=pltpu.VMEM)
SMEM_SPEC = pl.BlockSpec(memory_space=pltpu.SMEM)


def hier_line(line_level):
    points = 2**line_level
    matrix = np.zeros((points, points))
    matrix[0, 0] = 1.0
    for tier_rank in range(1, line_level + 1):
        stride = 2 ** (line_level - tier_rank)
        for entry_at in range(2 ** (tier_rank - 1), 2**tier_rank):
            node_at = (2 * (entry_at - 2 ** (tier_rank - 1)) + 1) * stride
            matrix[entry_at, node_at] += 1.0
            matrix[entry_at, (node_at - stride) % points] -= 0.5
            matrix[entry_at, (node_at + stride) % points] -= 0.5
    return matrix


def dehier_line(line_level):
    points = 2**line_level
    matrix = np.zeros((points, points))
    matrix[0, 0] = 1.0
    for tier_rank in range(1, line_level + 1):
        stride = 2 ** (line_level - tier_rank)
        for entry_at in range(2 ** (tier_rank - 1), 2**tier_rank):
            node_at = (2 * (entry_at - 2 ** (tier_rank - 1)) + 1) * stride
            matrix[node_at] = 0.5 * (
                matrix[(node_at - stride) % points] + matrix[(node_at + stride) % points]
            )
            matrix[node_at, entry_at] += 1.0
    return matrix


def row_tables():
    starts, widths, offsets = ([], [], [])
    running = 0
    for piece_level in range(LMIN, LMIN + NLEV):
        first_row = 0 if piece_level == LMIN else 2 ** (piece_level - 1)
        breadth = 2**LMIN if piece_level == LMIN else 2 ** (piece_level - 1)
        starts.append(first_row)
        widths.append(breadth)
        offsets.append(running)
        running += breadth * 2 ** (ROW_BITS - piece_level)
    padded = -(-running // 128) * 128
    forward, backward, embeds = ([], [], [])
    for shift_level in range(NLEV):
        first_level = LMIN + shift_level
        second_level = ROW_BITS - first_level
        tensor = np.kron(hier_line(first_level), hier_line(second_level))
        inverse = np.kron(dehier_line(first_level), dehier_line(second_level))
        order_list, place_list = ([], [])
        for slot_index in range(shift_level + 1):
            for second in range(2**second_level):
                for first_idx in range(starts[slot_index], starts[slot_index] + widths[slot_index]):
                    order_list.append(first_idx * 2**second_level + second)
                    place_list.append(
                        offsets[slot_index]
                        + second * widths[slot_index]
                        + first_idx
                        - starts[slot_index]
                    )
        embedding = np.zeros((padded, LANES))
        embedding[np.array(place_list), np.arange(LANES)] = 1.0
        forward.append(tensor[order_list].T)
        backward.append(inverse[:, order_list].T)
        embeds.append(embedding)
    stacked = np.concatenate([e.T for e in embeds], axis=0)
    cover = np.stack([e.sum(axis=1) for e in embeds])
    return np.stack(forward), np.stack(backward), stacked, cover, running, padded


def stencil_tables():
    tables = []
    for first_level in range(LMIN, LMIN + NLEV):
        inner = 2 ** (ROW_BITS - first_level)
        both = np.zeros((LANES, 2 * LANES))
        for row in range(LANES):
            base, pos = row - row % inner, row % inner
            both[row, row] -= 2.0 * (4**first_level + inner * inner)
            for sign in (1, -1):
                far = (row + sign * inner) % LANES
                near = base + (pos + sign) % inner
                both[far, row] += 4**first_level
                both[near, row] += inner * inner
                both[far, LANES + row] += sign
        tables.append(np.concatenate([both, both], axis=0))
    return np.stack(tables)


def tiers():
    found = []
    for tier_rank in range(1, CLEV + 1):
        stride = 2 ** (CLEV - tier_rank)
        for entry_at in range(2 ** (tier_rank - 1), 2**tier_rank):
            node_at = (2 * (entry_at - 2 ** (tier_rank - 1)) + 1) * stride
            found.append((entry_at, node_at, node_at - stride, (node_at + stride) % SIDE))
    return found


def split_dot(values, matrix):
    high = values.astype(jnp.bfloat16)
    low = (values - high.astype(jnp.float32)).astype(jnp.bfloat16)
    return jnp.dot(high, matrix, preferred_element_type=jnp.float32) + jnp.dot(
        low, matrix, preferred_element_type=jnp.float32
    )


def hier_lines(read, write):
    vals = [read(i) for i in range(SIDE)]
    write(0, vals[0])
    for entry_at, node_at, low_at, high_at in tiers():
        write(entry_at, vals[node_at] - 0.5 * (vals[low_at] + vals[high_at]))


def dehier_lines(read, write):
    vals = [None] * SIDE
    vals[0] = read(0)
    write(0, vals[0])
    for entry_at, node_at, low_at, high_at in tiers():
        vals[node_at] = read(entry_at) + 0.5 * (vals[low_at] + vals[high_at])
        write(node_at, vals[node_at])


def lines_first(op, buf, src, dst):
    for part in range(SIDE // 8):
        op(
            lambda i: buf[pl.ds(src + i * SIDE + part * 8, 8), :],
            lambda i, v: buf.__setitem__((pl.ds(dst + i * SIDE + part * 8, 8), slice(None)), v),
        )


def lines_second(op, buf, src, dst):
    for part in range(SIDE // 8):
        op(
            lambda i: buf[pl.ds(src + part * 8 * SIDE + i, 8, stride=SIDE), :],
            lambda i, v: buf.__setitem__(
                (pl.ds(dst + part * 8 * SIDE + i, 8, stride=SIDE), slice(None)), v
            ),
        )


def local_kernel(
    count, pre, post, in_map, out_map, tables, devices,
    levels, coeffs, assign, assign_next, owner, row_speed, x_ref, col_ref, stencil_ref, *rest,
):
    rest = list(rest)
    back_ref = rest.pop(0) if pre else None
    fwd_ref = rest.pop(0) if post else None
    out_ref = rest.pop(0)
    tab_ref = rest.pop(0) if tables else None
    buf, speed = rest
    cells = SIDE * SIDE
    block = cells // devices
    sections = devices // NLEV
    me = lax.axis_index("grid")

    if tables:
        def fill(g, carry):
            slot = (levels[g] - LMIN) * sections + g // NLEV
            tab_ref[slot] = assign[g]
            tab_ref[devices + slot] = assign_next[g]
            tab_ref[2 * devices + assign_next[g]] = slot
            tab_ref[3 * devices + slot] = coeffs[g]
            return carry
        lax.fori_loop(0, devices, fill, 0)

    own = lax.fori_loop(
        0, devices, lambda g, seen: jnp.where(assign[g] == me, g, seen), jnp.int32(0)
    )
    level = levels[own]
    inner = jnp.left_shift(jnp.int32(1), ROW_BITS - level)
    refine = jnp.left_shift(jnp.int32(1), level - LMIN)
    scale_one = jnp.left_shift(jnp.int32(1), level).astype(jnp.float32)
    dt = jnp.float32(time_step)
    for shift in range(1, NLEV):
        dt = jnp.where(level == LMIN + shift, jnp.float32(time_step / 2**shift), dt)
    k1 = dt * diffusivity
    k3 = dt * diffusivity * float(4**CLEV)
    k0 = 1.0 - 4.0 * k3

    lane = lax.broadcasted_iota(jnp.int32, (8, LANES), 1)
    inner_pos = jnp.bitwise_and(lane, inner - 1)
    sample_at = inner_pos * jnp.left_shift(jnp.int32(1), level - LMIN)
    row_factor = jnp.zeros((8, LANES), jnp.float32)
    for f in range(row_speed.shape[0]):
        row_factor = jnp.where(sample_at == f, row_speed[f], row_factor)
    row_factor = row_factor * (dt * 0.5 * scale_one)

    def speeds(i, carry):
        at = pl.multiple_of(i * 32, 32)
        speed[pl.ds(at, 32), :] = col_ref[pl.ds(at, 32), :] * jnp.concatenate([row_factor] * 4, axis=0)
        return carry
    lax.fori_loop(0, cells // 32, speeds, 0)

    if pre:
        def take(b, carry):
            buf[pl.ds(pl.multiple_of(b * block, block), block), :] = x_ref[owner[b] if in_map else b]
            return carry
        lax.fori_loop(0, devices, take, 0)
        weights = back_ref[level - LMIN]
        for at in range(0, cells, 256):
            buf[pl.ds(cells + at, 256), :] = split_dot(buf[pl.ds(at, 256), :], weights)
        lines_first(dehier_lines, buf, cells, 0)
        lines_second(dehier_lines, buf, 0, cells)
        start = 1
    else:
        buf[pl.ds(0, cells), :] = x_ref[0]
        start = 0

    group = 8
    rows = group * SIDE

    def substep(turn, parity):
        src = parity * cells
        dst = (1 - parity) * cells

        def slabs(i, carry):
            base = i * group
            at = pl.multiple_of(i * rows, rows)
            chunk = buf[pl.ds(pl.multiple_of(src + at, rows), rows), :]
            high = chunk.astype(jnp.bfloat16)
            low = (chunk - high.astype(jnp.float32)).astype(jnp.bfloat16)
            mixed = jnp.dot(
                jnp.concatenate([high, low], axis=1),
                stencil_ref[level - LMIN],
                preferred_element_type=jnp.float32,
            )
            cur = []
            for j in range(-1, group + 1):
                m = jnp.bitwise_and(base + j, SIDE - 1)
                cur.append(buf[pl.ds(pl.multiple_of(src + m * SIDE, SIDE), SIDE), :])
            for j in range(group):
                u = cur[j + 1]
                side = (pltpu.roll(u, 1, 0) + pltpu.roll(u, SIDE - 1, 0)) + (cur[j] + cur[j + 2])
                here = slice(j * SIDE, (j + 1) * SIDE)
                new = (k0 * u + k3 * side) + k1 * mixed[here, :LANES]
                new = new - speed[pl.ds(at + j * SIDE, SIDE), :] * mixed[here, LANES:]
                buf[pl.ds(pl.multiple_of(dst + (base + j) * SIDE, SIDE), SIDE), :] = new
            return carry

        lax.fori_loop(0, SIDE // group, slabs, 0)
        return 1 - parity

    final = lax.fori_loop(0, refine * count, substep, jnp.int32(start))

    if post:
        src, dst = start * cells, (1 - start) * cells
        lines_first(hier_lines, buf, src, dst)
        lines_second(hier_lines, buf, dst, src)
        weight = coeffs[own].astype(jnp.float32)
        weights = fwd_ref[level - LMIN]
        for at in range(0, cells, 256):
            buf[pl.ds(dst + at, 256), :] = weight * split_dot(buf[pl.ds(src + at, 256), :], weights)

        def give(b, carry):
            out_ref[owner[b] if out_map else b] = buf[
                pl.ds(pl.multiple_of(dst + b * block, block), block), :
            ]
            return carry
        lax.fori_loop(0, devices, give, 0)
    else:
        out_ref[0] = buf[pl.ds(pl.multiple_of(final * cells, cells), cells), :]


def exchange_kernel(
    source_row, keep, devices, parts, section_rows,
    tab, x_ref, embed_ref, take_ref, cover_ref, out_ref, *rest,
):
    rest = list(rest)
    keep_ref = rest.pop(0) if keep else None
    recvs = rest[:parts]
    wide, packs, send2, kept, sems = rest[parts:]
    block = x_ref.shape[1]
    part_cols = block // parts
    sections = devices // NLEV
    padded = cover_ref.shape[1]
    me = lax.axis_index("grid")
    half = devices // 2
    my_half = me // half
    my_place = lax.rem(me, half)

    barrier = pltpu.get_barrier_semaphore()

    def greet(i, carry):
        pl.semaphore_signal(
            barrier, inc=1, device_id={"grid": lax.rem(me + i, devices)}, device_id_type=MESH
        )
        return carry

    lax.fori_loop(1, devices, greet, 0)
    pl.semaphore_wait(barrier, devices - 1)

    def partner(across, j):
        return lax.rem(my_half + across, 2) * half + lax.rem(my_place + j, half)

    def copy_of(src, dst, phase, part, across, j):
        to = partner(across, j)
        cols = slice(part * part_cols, (part + 1) * part_cols)
        into = dst.at[me] if phase == 0 else dst.at[me, cols]
        base = 2 * (phase * parts + part)
        return pltpu.make_async_remote_copy(
            src_ref=src.at[to, cols],
            dst_ref=into,
            send_sem=sems.at[base, across * half + j],
            recv_sem=sems.at[base + 1, across * half + j],
            device_id={"grid": to},
            device_id_type=MESH,
        )

    def each_partner(act):
        for across in (1, 0):
            def body(j, carry, across=across):
                act(across, j)
                return carry
            lax.fori_loop(1 - across, half, body, 0)

    for part in range(parts):
        each_partner(lambda across, j: copy_of(x_ref, recvs[part], 0, part, across, j).start())
    for part in range(parts):
        recvs[part][me] = x_ref[me, part * part_cols : (part + 1) * part_cols]

    for part in range(parts):
        each_partner(lambda across, j: copy_of(x_ref, recvs[part], 0, part, across, j).wait())
        cols = slice(part * part_cols, (part + 1) * part_cols)

        def gather(q, carry):
            at = pl.multiple_of(q * part_cols, part_cols)
            for lev in range(NLEV):
                wide[pl.ds(at, part_cols), lev * LANES : (lev + 1) * LANES] = recvs[part][
                    tab[source_row * devices + lev * sections + q]
                ]
            return carry

        lax.fori_loop(0, sections, gather, 0)
        wide[:, 0:padded] = split_dot(wide[...], embed_ref[...])

        def divide(q, carry):
            denom = jnp.zeros((1, padded), jnp.float32)
            for lev in range(NLEV):
                denom = denom + cover_ref[lev : lev + 1, :] * tab[
                    3 * devices + lev * sections + q
                ].astype(jnp.float32)
            inverse = 1.0 / jnp.where(denom > 0.0, denom, 1.0)
            at = pl.multiple_of(q * part_cols, part_cols)
            value = wide[pl.ds(at, part_cols), 0:padded] * inverse
            wide[pl.ds(at, part_cols), 0:padded] = value
            if keep:
                kept[q, cols] = value
            return carry

        lax.fori_loop(0, sections, divide, 0)
        picked = split_dot(wide[:, 0:padded], take_ref[...])
        for lev in range(NLEV):
            packs[pl.ds(lev * sections, sections)] = picked[
                :, lev * LANES : (lev + 1) * LANES
            ].reshape(sections, part_cols, LANES)

        def answer(across, j):
            to = partner(across, j)
            send2[to, cols] = packs[tab[2 * devices + to]]
            copy_of(send2, out_ref, 1, part, across, j).start()

        each_partner(answer)
        out_ref[me, cols] = packs[tab[2 * devices + me]]

    if keep:
        for q in range(sections):
            keep_ref[:, q * section_rows : (q + 1) * section_rows] = kept[q, :, 0:section_rows]
    for part in range(parts):
        each_partner(lambda across, j: copy_of(send2, out_ref, 1, part, across, j).wait())


def local(start_field, col_speed, row_speed, levels, coeffs, assign_first, assign_second, owner_of):
    forward, backward, stacked, cover, section_rows, padded = row_tables()
    forward = jnp.asarray(forward, jnp.bfloat16)
    backward = jnp.asarray(backward, jnp.bfloat16)
    embed = jnp.asarray(stacked, jnp.bfloat16)
    take = jnp.asarray(stacked.T, jnp.bfloat16)
    cover = jnp.asarray(cover, jnp.float32)
    stencils = jnp.asarray(stencil_tables(), jnp.bfloat16)
    devices = lax.axis_size("grid")
    cells, lanes = start_field.shape[1:]
    block = cells // devices
    sections = devices // NLEV
    parts = 2 if block % 16 == 0 else 1
    columns = jnp.broadcast_to(col_speed[:, None], (cells, lanes))

    def stage(x, assign, assign_next, count, pre, post, in_map, out_map, tables):
        args = [levels, coeffs, assign, assign_next, owner_of, row_speed, x, columns, stencils]
        specs = [SMEM_SPEC] * 6 + [VMEM_SPEC] * 3
        if pre:
            args.append(backward)
            specs.append(VMEM_SPEC)
        if post:
            args.append(forward)
            specs.append(VMEM_SPEC)
        shape = (devices, block, lanes) if post else (1, cells, lanes)
        outs = [jax.ShapeDtypeStruct(shape, jnp.float32)]
        out_specs = [VMEM_SPEC]
        if tables:
            outs.append(jax.ShapeDtypeStruct((4 * devices,), jnp.int32))
            out_specs.append(SMEM_SPEC)
        return pl.pallas_call(
            functools.partial(local_kernel, count, pre, post, in_map, out_map, tables, devices),
            out_shape=outs,
            in_specs=specs,
            out_specs=out_specs,
            scratch_shapes=[
                pltpu.VMEM((2 * cells, lanes), jnp.float32),
                pltpu.VMEM((cells, lanes), jnp.float32),
            ],
        )(*args)

    def exchange(x, tab, source_row, keep, collective_id):
        outs = [jax.ShapeDtypeStruct((devices, block, lanes), jnp.float32)]
        if keep:
            outs.append(jax.ShapeDtypeStruct((block, sections * section_rows), jnp.float32))
        return pl.pallas_call(
            functools.partial(exchange_kernel, source_row, keep, devices, parts, section_rows),
            out_shape=outs,
            in_specs=[SMEM_SPEC] + [VMEM_SPEC] * 4,
            out_specs=[VMEM_SPEC] * len(outs),
            scratch_shapes=[
            ]
            + [pltpu.VMEM((devices, block // parts, lanes), jnp.float32)] * parts
            + [
                pltpu.VMEM((sections * block // parts, NLEV * lanes), jnp.float32),
                pltpu.VMEM((devices, block // parts, lanes), jnp.float32),
                pltpu.VMEM((devices, block, lanes), jnp.float32),
                pltpu.VMEM((sections, block, padded), jnp.float32),
                pltpu.SemaphoreType.DMA((4 * parts, devices)),
            ],
            compiler_params=pltpu.CompilerParams(
                collective_id=collective_id, has_side_effects=True
            ),
        )(tab, x, embed, take, cover)

    outgoing, tab = stage(
        start_field, assign_first, assign_second, STEPS, False, True, False, False, True
    )
    (restricted,) = exchange(outgoing, tab, 0, False, 0)
    (outgoing,) = stage(
        restricted, assign_second, assign_second, STEPS, True, True, False, True, False
    )
    restricted, combined = exchange(outgoing, tab, 1, True, 1)
    (final,) = stage(restricted, assign_second, assign_second, 1, True, False, True, False, False)
    return combined, final


def solution(mesh):
    placed = (
        P(("groups", "grid"), None, None),
        P(),
        P(),
        P("groups"),
        P("groups"),
        P("groups"),
        P("groups"),
        P("groups"),
    )
    return jax.shard_map(
        local,
        mesh=mesh,
        in_specs=placed,
        out_specs=(P(("groups", "grid"), None), P(("groups", "grid"), None, None)),
        check_vma=False,
    )
```

```python
import functools

import jax
import jax.numpy as jnp
import numpy as np
from jax import lax
from jax.experimental import pallas as pl
from jax.experimental.pallas import tpu as pltpu
from jax.sharding import PartitionSpec as P

LMIN = 2
NLEV = 4
CLEV = 5
STEPS = 2
SIDE = 2**CLEV
ROW_BITS = 2 * LMIN + NLEV - 1
LANES = 2**ROW_BITS

time_step = 0.02
diffusivity = 0.0024
MESH = pl.DeviceIdType.MESH
VMEM_SPEC = pl.BlockSpec(memory_space=pltpu.VMEM)
SMEM_SPEC = pl.BlockSpec(memory_space=pltpu.SMEM)


def hier_line(line_level):
    points = 2**line_level
    matrix = np.zeros((points, points))
    matrix[0, 0] = 1.0
    for tier_rank in range(1, line_level + 1):
        stride = 2 ** (line_level - tier_rank)
        for entry_at in range(2 ** (tier_rank - 1), 2**tier_rank):
            node_at = (2 * (entry_at - 2 ** (tier_rank - 1)) + 1) * stride
            matrix[entry_at, node_at] += 1.0
            matrix[entry_at, (node_at - stride) % points] -= 0.5
            matrix[entry_at, (node_at + stride) % points] -= 0.5
    return matrix


def dehier_line(line_level):
    points = 2**line_level
    matrix = np.zeros((points, points))
    matrix[0, 0] = 1.0
    for tier_rank in range(1, line_level + 1):
        stride = 2 ** (line_level - tier_rank)
        for entry_at in range(2 ** (tier_rank - 1), 2**tier_rank):
            node_at = (2 * (entry_at - 2 ** (tier_rank - 1)) + 1) * stride
            matrix[node_at] = 0.5 * (
                matrix[(node_at - stride) % points] + matrix[(node_at + stride) % points]
            )
            matrix[node_at, entry_at] += 1.0
    return matrix


def row_tables():
    starts, widths, offsets = ([], [], [])
    running = 0
    for piece_level in range(LMIN, LMIN + NLEV):
        first_row = 0 if piece_level == LMIN else 2 ** (piece_level - 1)
        breadth = 2**LMIN if piece_level == LMIN else 2 ** (piece_level - 1)
        starts.append(first_row)
        widths.append(breadth)
        offsets.append(running)
        running += breadth * 2 ** (ROW_BITS - piece_level)
    padded = -(-running // 128) * 128
    forward, backward, embeds = ([], [], [])
    for shift_level in range(NLEV):
        first_level = LMIN + shift_level
        second_level = ROW_BITS - first_level
        tensor = np.kron(hier_line(first_level), hier_line(second_level))
        inverse = np.kron(dehier_line(first_level), dehier_line(second_level))
        order_list, place_list = ([], [])
        for slot_index in range(shift_level + 1):
            for second in range(2**second_level):
                for first_idx in range(starts[slot_index], starts[slot_index] + widths[slot_index]):
                    order_list.append(first_idx * 2**second_level + second)
                    place_list.append(
                        offsets[slot_index]
                        + second * widths[slot_index]
                        + first_idx
                        - starts[slot_index]
                    )
        embedding = np.zeros((padded, LANES))
        embedding[np.array(place_list), np.arange(LANES)] = 1.0
        forward.append(tensor[order_list].T)
        backward.append(inverse[:, order_list].T)
        embeds.append(embedding)
    stacked = np.concatenate([e.T for e in embeds], axis=0)
    cover = np.stack([e.sum(axis=1) for e in embeds])
    return np.stack(forward), np.stack(backward), stacked, cover, running, padded


def stencil_tables():
    tables = []
    for first_level in range(LMIN, LMIN + NLEV):
        inner = 2 ** (ROW_BITS - first_level)
        both = np.zeros((LANES, 2 * LANES))
        for row in range(LANES):
            base, pos = row - row % inner, row % inner
            both[row, row] -= 2.0 * (4**first_level + inner * inner)
            for sign in (1, -1):
                far = (row + sign * inner) % LANES
                near = base + (pos + sign) % inner
                both[far, row] += 4**first_level
                both[near, row] += inner * inner
                both[far, LANES + row] += sign
        tables.append(np.concatenate([both, both], axis=0))
    return np.stack(tables)


def tiers():
    found = []
    for tier_rank in range(1, CLEV + 1):
        stride = 2 ** (CLEV - tier_rank)
        for entry_at in range(2 ** (tier_rank - 1), 2**tier_rank):
            node_at = (2 * (entry_at - 2 ** (tier_rank - 1)) + 1) * stride
            found.append((entry_at, node_at, node_at - stride, (node_at + stride) % SIDE))
    return found


def split_dot(values, matrix):
    high = values.astype(jnp.bfloat16)
    low = (values - high.astype(jnp.float32)).astype(jnp.bfloat16)
    return jnp.dot(high, matrix, preferred_element_type=jnp.float32) + jnp.dot(
        low, matrix, preferred_element_type=jnp.float32
    )


def hier_lines(read, write):
    vals = [read(i) for i in range(SIDE)]
    write(0, vals[0])
    for entry_at, node_at, low_at, high_at in tiers():
        write(entry_at, vals[node_at] - 0.5 * (vals[low_at] + vals[high_at]))


def dehier_lines(read, write):
    vals = [None] * SIDE
    vals[0] = read(0)
    write(0, vals[0])
    for entry_at, node_at, low_at, high_at in tiers():
        vals[node_at] = read(entry_at) + 0.5 * (vals[low_at] + vals[high_at])
        write(node_at, vals[node_at])


def lines_first(op, buf, src, dst):
    for part in range(SIDE // 8):
        op(
            lambda i: buf[pl.ds(src + i * SIDE + part * 8, 8), :],
            lambda i, v: buf.__setitem__((pl.ds(dst + i * SIDE + part * 8, 8), slice(None)), v),
        )


def lines_second(op, buf, src, dst):
    for part in range(SIDE // 8):
        op(
            lambda i: buf[pl.ds(src + part * 8 * SIDE + i, 8, stride=SIDE), :],
            lambda i, v: buf.__setitem__(
                (pl.ds(dst + part * 8 * SIDE + i, 8, stride=SIDE), slice(None)), v
            ),
        )


def local_kernel(
    count, pre, post, in_map, out_map, tables, devices,
    levels, coeffs, assign, assign_next, owner, row_speed, x_ref, col_ref, stencil_ref, *rest,
):
    rest = list(rest)
    back_ref = rest.pop(0) if pre else None
    fwd_ref = rest.pop(0) if post else None
    out_ref = rest.pop(0)
    tab_ref = rest.pop(0) if tables else None
    buf, speed = rest
    cells = SIDE * SIDE
    block = cells // devices
    sections = devices // NLEV
    me = lax.axis_index("grid")

    if tables:
        def fill(g, carry):
            slot = (levels[g] - LMIN) * sections + g // NLEV
            tab_ref[slot] = assign[g]
            tab_ref[devices + slot] = assign_next[g]
            tab_ref[2 * devices + assign_next[g]] = slot
            tab_ref[3 * devices + slot] = coeffs[g]
            return carry
        lax.fori_loop(0, devices, fill, 0)

    own = lax.fori_loop(
        0, devices, lambda g, seen: jnp.where(assign[g] == me, g, seen), jnp.int32(0)
    )
    level = levels[own]
    inner = jnp.left_shift(jnp.int32(1), ROW_BITS - level)
    refine = jnp.left_shift(jnp.int32(1), level - LMIN)
    scale_one = jnp.left_shift(jnp.int32(1), level).astype(jnp.float32)
    dt = jnp.float32(time_step)
    for shift in range(1, NLEV):
        dt = jnp.where(level == LMIN + shift, jnp.float32(time_step / 2**shift), dt)
    k1 = dt * diffusivity
    k3 = dt * diffusivity * float(4**CLEV)
    k0 = 1.0 - 4.0 * k3

    lane = lax.broadcasted_iota(jnp.int32, (8, LANES), 1)
    inner_pos = jnp.bitwise_and(lane, inner - 1)
    sample_at = inner_pos * jnp.left_shift(jnp.int32(1), level - LMIN)
    row_factor = jnp.zeros((8, LANES), jnp.float32)
    for f in range(row_speed.shape[0]):
        row_factor = jnp.where(sample_at == f, row_speed[f], row_factor)
    row_factor = row_factor * (dt * 0.5 * scale_one)

    for at in range(0, cells, 256):
        speed[pl.ds(at, 256), :] = lax.dot_general(
            col_ref[:, at : at + 256],
            row_factor[0:1, :],
            (((0,), (0,)), ((), ())),
            precision=lax.Precision.HIGHEST,
            preferred_element_type=jnp.float32,
        )

    if pre:
        def take(b, carry):
            buf[pl.ds(pl.multiple_of(b * block, block), block), :] = x_ref[owner[b] if in_map else b]
            return carry
        lax.fori_loop(0, devices, take, 0)
        weights = back_ref[level - LMIN]
        for at in range(0, cells, 256):
            buf[pl.ds(cells + at, 256), :] = split_dot(buf[pl.ds(at, 256), :], weights)
        lines_first(dehier_lines, buf, cells, 0)
        lines_second(dehier_lines, buf, 0, cells)
        start = 1
    else:
        buf[pl.ds(0, cells), :] = x_ref[0]
        start = 0

    group = 16
    rows = group * SIDE

    def substep(turn, parity):
        src = parity * cells
        dst = (1 - parity) * cells

        def slabs(i, carry):
            base = i * group
            at = pl.multiple_of(i * rows, rows)
            chunk = buf[pl.ds(pl.multiple_of(src + at, rows), rows), :]
            high = chunk.astype(jnp.bfloat16)
            low = (chunk - high.astype(jnp.float32)).astype(jnp.bfloat16)
            mixed = jnp.dot(
                jnp.concatenate([high, low], axis=1),
                stencil_ref[level - LMIN],
                preferred_element_type=jnp.float32,
            )
            cur = []
            for j in range(-1, group + 1):
                m = jnp.bitwise_and(base + j, SIDE - 1)
                cur.append(buf[pl.ds(pl.multiple_of(src + m * SIDE, SIDE), SIDE), :])
            for j in range(group):
                u = cur[j + 1]
                side = (pltpu.roll(u, 1, 0) + pltpu.roll(u, SIDE - 1, 0)) + (cur[j] + cur[j + 2])
                here = slice(j * SIDE, (j + 1) * SIDE)
                new = (k0 * u + k3 * side) + k1 * mixed[here, :LANES]
                new = new - speed[pl.ds(at + j * SIDE, SIDE), :] * mixed[here, LANES:]
                buf[pl.ds(pl.multiple_of(dst + (base + j) * SIDE, SIDE), SIDE), :] = new
            return carry

        lax.fori_loop(0, SIDE // group, slabs, 0)
        return 1 - parity

    final = lax.fori_loop(0, refine * count, substep, jnp.int32(start))

    if post:
        src, dst = start * cells, (1 - start) * cells
        lines_first(hier_lines, buf, src, dst)
        lines_second(hier_lines, buf, dst, src)
        weight = coeffs[own].astype(jnp.float32)
        weights = fwd_ref[level - LMIN]
        for at in range(0, cells, 256):
            buf[pl.ds(dst + at, 256), :] = weight * split_dot(buf[pl.ds(src + at, 256), :], weights)

        def give(b, carry):
            out_ref[owner[b] if out_map else b] = buf[
                pl.ds(pl.multiple_of(dst + b * block, block), block), :
            ]
            return carry
        lax.fori_loop(0, devices, give, 0)
    else:
        out_ref[0] = buf[pl.ds(pl.multiple_of(final * cells, cells), cells), :]


def exchange_kernel(
    source_row, keep, devices, parts, section_rows,
    tab, x_ref, embed_ref, take_ref, cover_ref, out_ref, *rest,
):
    rest = list(rest)
    keep_ref = rest.pop(0) if keep else None
    recvs = rest[:parts]
    wide, packs, send2, kept, sems = rest[parts:]
    block = x_ref.shape[1]
    part_cols = block // parts
    sections = devices // NLEV
    padded = cover_ref.shape[1]
    me = lax.axis_index("grid")
    half = devices // 2
    my_half = me // half
    my_place = lax.rem(me, half)

    barrier = pltpu.get_barrier_semaphore()

    def greet(i, carry):
        pl.semaphore_signal(
            barrier, inc=1, device_id={"grid": lax.rem(me + i, devices)}, device_id_type=MESH
        )
        return carry

    lax.fori_loop(1, devices, greet, 0)
    pl.semaphore_wait(barrier, devices - 1)

    def partner(across, j):
        return lax.rem(my_half + across, 2) * half + lax.rem(my_place + j, half)

    def copy_of(src, dst, phase, part, across, j):
        to = partner(across, j)
        cols = slice(part * part_cols, (part + 1) * part_cols)
        into = dst.at[me] if phase == 0 else dst.at[me, cols]
        base = 2 * (phase * parts + part)
        return pltpu.make_async_remote_copy(
            src_ref=src.at[to, cols],
            dst_ref=into,
            send_sem=sems.at[base, across * half + j],
            recv_sem=sems.at[base + 1, across * half + j],
            device_id={"grid": to},
            device_id_type=MESH,
        )

    def each_partner(act):
        for across in (1, 0):
            def body(j, carry, across=across):
                act(across, j)
                return carry
            lax.fori_loop(1 - across, half, body, 0)

    for part in range(parts):
        each_partner(lambda across, j: copy_of(x_ref, recvs[part], 0, part, across, j).start())
    for part in range(parts):
        recvs[part][me] = x_ref[me, part * part_cols : (part + 1) * part_cols]

    for part in range(parts):
        each_partner(lambda across, j: copy_of(x_ref, recvs[part], 0, part, across, j).wait())
        cols = slice(part * part_cols, (part + 1) * part_cols)

        def gather(q, carry):
            at = pl.multiple_of(q * part_cols, part_cols)
            for lev in range(NLEV):
                wide[pl.ds(at, part_cols), lev * LANES : (lev + 1) * LANES] = recvs[part][
                    tab[source_row * devices + lev * sections + q]
                ]
            return carry

        lax.fori_loop(0, sections, gather, 0)
        wide[:, 0:padded] = split_dot(wide[...], embed_ref[...])

        def divide(q, carry):
            denom = jnp.zeros((1, padded), jnp.float32)
            for lev in range(NLEV):
                denom = denom + cover_ref[lev : lev + 1, :] * tab[
                    3 * devices + lev * sections + q
                ].astype(jnp.float32)
            inverse = 1.0 / jnp.where(denom > 0.0, denom, 1.0)
            at = pl.multiple_of(q * part_cols, part_cols)
            value = wide[pl.ds(at, part_cols), 0:padded] * inverse
            wide[pl.ds(at, part_cols), 0:padded] = value
            if keep:
                kept[q, cols] = value
            return carry

        lax.fori_loop(0, sections, divide, 0)
        picked = split_dot(wide[:, 0:padded], take_ref[...])
        for lev in range(NLEV):
            packs[pl.ds(lev * sections, sections)] = picked[
                :, lev * LANES : (lev + 1) * LANES
            ].reshape(sections, part_cols, LANES)

        def answer(across, j):
            to = partner(across, j)
            send2[to, cols] = packs[tab[2 * devices + to]]
            copy_of(send2, out_ref, 1, part, across, j).start()

        each_partner(answer)
        out_ref[me, cols] = packs[tab[2 * devices + me]]

    if keep:
        for q in range(sections):
            keep_ref[:, q * section_rows : (q + 1) * section_rows] = kept[q, :, 0:section_rows]
    for part in range(parts):
        each_partner(lambda across, j: copy_of(send2, out_ref, 1, part, across, j).wait())


def local(start_field, col_speed, row_speed, levels, coeffs, assign_first, assign_second, owner_of):
    forward, backward, stacked, cover, section_rows, padded = row_tables()
    forward = jnp.asarray(forward, jnp.bfloat16)
    backward = jnp.asarray(backward, jnp.bfloat16)
    embed = jnp.asarray(stacked, jnp.bfloat16)
    take = jnp.asarray(stacked.T, jnp.bfloat16)
    cover = jnp.asarray(cover, jnp.float32)
    stencils = jnp.asarray(stencil_tables(), jnp.bfloat16)
    devices = lax.axis_size("grid")
    cells, lanes = start_field.shape[1:]
    block = cells // devices
    sections = devices // NLEV
    parts = 2 if block % 16 == 0 else 1
    columns = col_speed.reshape(1, cells)

    def stage(x, assign, assign_next, count, pre, post, in_map, out_map, tables):
        args = [levels, coeffs, assign, assign_next, owner_of, row_speed, x, columns, stencils]
        specs = [SMEM_SPEC] * 6 + [VMEM_SPEC] * 3
        if pre:
            args.append(backward)
            specs.append(VMEM_SPEC)
        if post:
            args.append(forward)
            specs.append(VMEM_SPEC)
        shape = (devices, block, lanes) if post else (1, cells, lanes)
        outs = [jax.ShapeDtypeStruct(shape, jnp.float32)]
        out_specs = [VMEM_SPEC]
        if tables:
            outs.append(jax.ShapeDtypeStruct((4 * devices,), jnp.int32))
            out_specs.append(SMEM_SPEC)
        return pl.pallas_call(
            functools.partial(local_kernel, count, pre, post, in_map, out_map, tables, devices),
            out_shape=outs,
            in_specs=specs,
            out_specs=out_specs,
            scratch_shapes=[
                pltpu.VMEM((2 * cells, lanes), jnp.float32),
                pltpu.VMEM((cells, lanes), jnp.float32),
            ],
        )(*args)

    def exchange(x, tab, source_row, keep, collective_id):
        outs = [jax.ShapeDtypeStruct((devices, block, lanes), jnp.float32)]
        if keep:
            outs.append(jax.ShapeDtypeStruct((block, sections * section_rows), jnp.float32))
        return pl.pallas_call(
            functools.partial(exchange_kernel, source_row, keep, devices, parts, section_rows),
            out_shape=outs,
            in_specs=[SMEM_SPEC] + [VMEM_SPEC] * 4,
            out_specs=[VMEM_SPEC] * len(outs),
            scratch_shapes=[
            ]
            + [pltpu.VMEM((devices, block // parts, lanes), jnp.float32)] * parts
            + [
                pltpu.VMEM((sections * block // parts, NLEV * lanes), jnp.float32),
                pltpu.VMEM((devices, block // parts, lanes), jnp.float32),
                pltpu.VMEM((devices, block, lanes), jnp.float32),
                pltpu.VMEM((sections, block, padded), jnp.float32),
                pltpu.SemaphoreType.DMA((4 * parts, devices)),
            ],
            compiler_params=pltpu.CompilerParams(
                collective_id=collective_id, has_side_effects=True
            ),
        )(tab, x, embed, take, cover)

    outgoing, tab = stage(
        start_field, assign_first, assign_second, STEPS, False, True, False, False, True
    )
    (restricted,) = exchange(outgoing, tab, 0, False, 0)
    (outgoing,) = stage(
        restricted, assign_second, assign_second, STEPS, True, True, False, True, False
    )
    restricted, combined = exchange(outgoing, tab, 1, True, 1)
    (final,) = stage(restricted, assign_second, assign_second, 1, True, False, True, False, False)
    return combined, final


def solution(mesh):
    placed = (
        P(("groups", "grid"), None, None),
        P(),
        P(),
        P("groups"),
        P("groups"),
        P("groups"),
        P("groups"),
        P("groups"),
    )
    return jax.shard_map(
        local,
        mesh=mesh,
        in_specs=placed,
        out_specs=(P(("groups", "grid"), None), P(("groups", "grid"), None, None)),
        check_vma=False,
    )
```

```python
import functools

import jax
import jax.numpy as jnp
import numpy as np
from jax import lax
from jax.experimental import pallas as pl
from jax.experimental.pallas import tpu as pltpu
from jax.sharding import PartitionSpec as P

LMIN = 2
NLEV = 4
CLEV = 5
STEPS = 2
SIDE = 2**CLEV
ROW_BITS = 2 * LMIN + NLEV - 1
LANES = 2**ROW_BITS

time_step = 0.02
diffusivity = 0.0024
MESH = pl.DeviceIdType.MESH
VMEM_SPEC = pl.BlockSpec(memory_space=pltpu.VMEM)
SMEM_SPEC = pl.BlockSpec(memory_space=pltpu.SMEM)


def hier_line(line_level):
    points = 2**line_level
    matrix = np.zeros((points, points))
    matrix[0, 0] = 1.0
    for tier_rank in range(1, line_level + 1):
        stride = 2 ** (line_level - tier_rank)
        for entry_at in range(2 ** (tier_rank - 1), 2**tier_rank):
            node_at = (2 * (entry_at - 2 ** (tier_rank - 1)) + 1) * stride
            matrix[entry_at, node_at] += 1.0
            matrix[entry_at, (node_at - stride) % points] -= 0.5
            matrix[entry_at, (node_at + stride) % points] -= 0.5
    return matrix


def dehier_line(line_level):
    points = 2**line_level
    matrix = np.zeros((points, points))
    matrix[0, 0] = 1.0
    for tier_rank in range(1, line_level + 1):
        stride = 2 ** (line_level - tier_rank)
        for entry_at in range(2 ** (tier_rank - 1), 2**tier_rank):
            node_at = (2 * (entry_at - 2 ** (tier_rank - 1)) + 1) * stride
            matrix[node_at] = 0.5 * (
                matrix[(node_at - stride) % points] + matrix[(node_at + stride) % points]
            )
            matrix[node_at, entry_at] += 1.0
    return matrix


def row_tables():
    starts, widths, offsets = ([], [], [])
    running = 0
    for piece_level in range(LMIN, LMIN + NLEV):
        first_row = 0 if piece_level == LMIN else 2 ** (piece_level - 1)
        breadth = 2**LMIN if piece_level == LMIN else 2 ** (piece_level - 1)
        starts.append(first_row)
        widths.append(breadth)
        offsets.append(running)
        running += breadth * 2 ** (ROW_BITS - piece_level)
    padded = -(-running // 128) * 128
    forward, backward, embeds = ([], [], [])
    for shift_level in range(NLEV):
        first_level = LMIN + shift_level
        second_level = ROW_BITS - first_level
        tensor = np.kron(hier_line(first_level), hier_line(second_level))
        inverse = np.kron(dehier_line(first_level), dehier_line(second_level))
        order_list, place_list = ([], [])
        for slot_index in range(shift_level + 1):
            for second in range(2**second_level):
                for first_idx in range(starts[slot_index], starts[slot_index] + widths[slot_index]):
                    order_list.append(first_idx * 2**second_level + second)
                    place_list.append(
                        offsets[slot_index]
                        + second * widths[slot_index]
                        + first_idx
                        - starts[slot_index]
                    )
        embedding = np.zeros((padded, LANES))
        embedding[np.array(place_list), np.arange(LANES)] = 1.0
        forward.append(tensor[order_list].T)
        backward.append(inverse[:, order_list].T)
        embeds.append(embedding)
    stacked = np.concatenate([e.T for e in embeds], axis=0)
    cover = np.stack([e.sum(axis=1) for e in embeds])
    return np.stack(forward), np.stack(backward), stacked, cover, running, padded


def stencil_tables():
    tables = []
    for first_level in range(LMIN, LMIN + NLEV):
        inner = 2 ** (ROW_BITS - first_level)
        both = np.zeros((LANES, 2 * LANES))
        for row in range(LANES):
            base, pos = row - row % inner, row % inner
            both[row, row] -= 2.0 * (4**first_level + inner * inner)
            for sign in (1, -1):
                far = (row + sign * inner) % LANES
                near = base + (pos + sign) % inner
                both[far, row] += 4**first_level
                both[near, row] += inner * inner
                both[far, LANES + row] += sign
        tables.append(np.concatenate([both, both], axis=0))
    return np.stack(tables)


def tiers():
    found = []
    for tier_rank in range(1, CLEV + 1):
        stride = 2 ** (CLEV - tier_rank)
        for entry_at in range(2 ** (tier_rank - 1), 2**tier_rank):
            node_at = (2 * (entry_at - 2 ** (tier_rank - 1)) + 1) * stride
            found.append((entry_at, node_at, node_at - stride, (node_at + stride) % SIDE))
    return found


def split_dot(values, matrix):
    high = values.astype(jnp.bfloat16)
    low = (values - high.astype(jnp.float32)).astype(jnp.bfloat16)
    return jnp.dot(high, matrix, preferred_element_type=jnp.float32) + jnp.dot(
        low, matrix, preferred_element_type=jnp.float32
    )


def hier_lines(read, write):
    vals = [read(i) for i in range(SIDE)]
    write(0, vals[0])
    for entry_at, node_at, low_at, high_at in tiers():
        write(entry_at, vals[node_at] - 0.5 * (vals[low_at] + vals[high_at]))


def dehier_lines(read, write):
    vals = [None] * SIDE
    vals[0] = read(0)
    write(0, vals[0])
    for entry_at, node_at, low_at, high_at in tiers():
        vals[node_at] = read(entry_at) + 0.5 * (vals[low_at] + vals[high_at])
        write(node_at, vals[node_at])


def lines_first(op, buf, src, dst):
    for part in range(SIDE // 8):
        op(
            lambda i: buf[pl.ds(src + i * SIDE + part * 8, 8), :],
            lambda i, v: buf.__setitem__((pl.ds(dst + i * SIDE + part * 8, 8), slice(None)), v),
        )


def lines_second(op, buf, src, dst):
    for part in range(SIDE // 8):
        op(
            lambda i: buf[pl.ds(src + part * 8 * SIDE + i, 8, stride=SIDE), :],
            lambda i, v: buf.__setitem__(
                (pl.ds(dst + part * 8 * SIDE + i, 8, stride=SIDE), slice(None)), v
            ),
        )


def local_kernel(
    count, pre, post, in_map, out_map, tables, devices,
    levels, coeffs, assign, assign_next, owner, row_speed, x_ref, col_ref, stencil_ref, *rest,
):
    rest = list(rest)
    back_ref = rest.pop(0) if pre else None
    fwd_ref = rest.pop(0) if post else None
    out_ref = rest.pop(0)
    tab_ref = rest.pop(0) if tables else None
    buf, speed = rest
    cells = SIDE * SIDE
    block = cells // devices
    sections = devices // NLEV
    me = lax.axis_index("grid")

    if tables:
        def fill(g, carry):
            slot = (levels[g] - LMIN) * sections + g // NLEV
            tab_ref[slot] = assign[g]
            tab_ref[devices + slot] = assign_next[g]
            tab_ref[2 * devices + assign_next[g]] = slot
            tab_ref[3 * devices + slot] = coeffs[g]
            return carry
        lax.fori_loop(0, devices, fill, 0)

    own = lax.fori_loop(
        0, devices, lambda g, seen: jnp.where(assign[g] == me, g, seen), jnp.int32(0)
    )
    level = levels[own]
    inner = jnp.left_shift(jnp.int32(1), ROW_BITS - level)
    refine = jnp.left_shift(jnp.int32(1), level - LMIN)
    scale_one = jnp.left_shift(jnp.int32(1), level).astype(jnp.float32)
    dt = jnp.float32(time_step)
    for shift in range(1, NLEV):
        dt = jnp.where(level == LMIN + shift, jnp.float32(time_step / 2**shift), dt)
    k1 = dt * diffusivity
    k3 = dt * diffusivity * float(4**CLEV)
    k0 = 1.0 - 4.0 * k3

    lane = lax.broadcasted_iota(jnp.int32, (8, LANES), 1)
    inner_pos = jnp.bitwise_and(lane, inner - 1)
    sample_at = inner_pos * jnp.left_shift(jnp.int32(1), level - LMIN)
    row_factor = jnp.zeros((8, LANES), jnp.float32)
    for f in range(row_speed.shape[0]):
        row_factor = jnp.where(sample_at == f, row_speed[f], row_factor)
    row_factor = row_factor * (dt * 0.5 * scale_one)

    for at in range(0, cells, 256):
        speed[pl.ds(at, 256), :] = lax.dot_general(
            col_ref[:, at : at + 256],
            row_factor[0:1, :],
            (((0,), (0,)), ((), ())),
            precision=lax.Precision.HIGHEST,
            preferred_element_type=jnp.float32,
        )

    if pre:
        def take(b, carry):
            buf[pl.ds(pl.multiple_of(b * block, block), block), :] = x_ref[owner[b] if in_map else b]
            return carry
        lax.fori_loop(0, devices, take, 0)
        weights = back_ref[level - LMIN]
        for at in range(0, cells, 256):
            buf[pl.ds(cells + at, 256), :] = split_dot(buf[pl.ds(at, 256), :], weights)
        lines_first(dehier_lines, buf, cells, 0)
        lines_second(dehier_lines, buf, 0, cells)
        start = 1
    else:
        buf[pl.ds(0, cells), :] = x_ref[0]
        start = 0

    group = 32
    rows = group * SIDE

    def substep(turn, parity):
        src = parity * cells
        dst = (1 - parity) * cells

        def slabs(i, carry):
            base = i * group
            at = pl.multiple_of(i * rows, rows)
            chunk = buf[pl.ds(pl.multiple_of(src + at, rows), rows), :]
            high = chunk.astype(jnp.bfloat16)
            low = (chunk - high.astype(jnp.float32)).astype(jnp.bfloat16)
            mixed = jnp.dot(
                jnp.concatenate([high, low], axis=1),
                stencil_ref[level - LMIN],
                preferred_element_type=jnp.float32,
            )
            cur = []
            for j in range(-1, group + 1):
                m = jnp.bitwise_and(base + j, SIDE - 1)
                cur.append(buf[pl.ds(pl.multiple_of(src + m * SIDE, SIDE), SIDE), :])
            for j in range(group):
                u = cur[j + 1]
                side = (pltpu.roll(u, 1, 0) + pltpu.roll(u, SIDE - 1, 0)) + (cur[j] + cur[j + 2])
                here = slice(j * SIDE, (j + 1) * SIDE)
                new = (k0 * u + k3 * side) + k1 * mixed[here, :LANES]
                new = new - speed[pl.ds(at + j * SIDE, SIDE), :] * mixed[here, LANES:]
                buf[pl.ds(pl.multiple_of(dst + (base + j) * SIDE, SIDE), SIDE), :] = new
            return carry

        lax.fori_loop(0, SIDE // group, slabs, 0)
        return 1 - parity

    final = lax.fori_loop(0, refine * count, substep, jnp.int32(start))

    if post:
        src, dst = start * cells, (1 - start) * cells
        lines_first(hier_lines, buf, src, dst)
        lines_second(hier_lines, buf, dst, src)
        weight = coeffs[own].astype(jnp.float32)
        weights = fwd_ref[level - LMIN]
        for at in range(0, cells, 256):
            buf[pl.ds(dst + at, 256), :] = weight * split_dot(buf[pl.ds(src + at, 256), :], weights)

        def give(b, carry):
            out_ref[owner[b] if out_map else b] = buf[
                pl.ds(pl.multiple_of(dst + b * block, block), block), :
            ]
            return carry
        lax.fori_loop(0, devices, give, 0)
    else:
        out_ref[0] = buf[pl.ds(pl.multiple_of(final * cells, cells), cells), :]


def exchange_kernel(
    source_row, keep, devices, parts, section_rows,
    tab, x_ref, embed_ref, take_ref, cover_ref, out_ref, *rest,
):
    rest = list(rest)
    keep_ref = rest.pop(0) if keep else None
    recvs = rest[:parts]
    wide, packs, send2, kept, sems = rest[parts:]
    block = x_ref.shape[1]
    part_cols = block // parts
    sections = devices // NLEV
    padded = cover_ref.shape[1]
    me = lax.axis_index("grid")
    half = devices // 2
    my_half = me // half
    my_place = lax.rem(me, half)

    barrier = pltpu.get_barrier_semaphore()

    def greet(i, carry):
        pl.semaphore_signal(
            barrier, inc=1, device_id={"grid": lax.rem(me + i, devices)}, device_id_type=MESH
        )
        return carry

    lax.fori_loop(1, devices, greet, 0)
    pl.semaphore_wait(barrier, devices - 1)

    def partner(across, j):
        return lax.rem(my_half + across, 2) * half + lax.rem(my_place + j, half)

    def copy_of(src, dst, phase, part, across, j):
        to = partner(across, j)
        cols = slice(part * part_cols, (part + 1) * part_cols)
        into = dst.at[me] if phase == 0 else dst.at[me, cols]
        base = 2 * (phase * parts + part)
        return pltpu.make_async_remote_copy(
            src_ref=src.at[to, cols],
            dst_ref=into,
            send_sem=sems.at[base, across * half + j],
            recv_sem=sems.at[base + 1, across * half + j],
            device_id={"grid": to},
            device_id_type=MESH,
        )

    def each_partner(act):
        for across in (1, 0):
            def body(j, carry, across=across):
                act(across, j)
                return carry
            lax.fori_loop(1 - across, half, body, 0)

    for part in range(parts):
        each_partner(lambda across, j: copy_of(x_ref, recvs[part], 0, part, across, j).start())
    for part in range(parts):
        recvs[part][me] = x_ref[me, part * part_cols : (part + 1) * part_cols]

    for part in range(parts):
        each_partner(lambda across, j: copy_of(x_ref, recvs[part], 0, part, across, j).wait())
        cols = slice(part * part_cols, (part + 1) * part_cols)

        def gather(q, carry):
            at = pl.multiple_of(q * part_cols, part_cols)
            for lev in range(NLEV):
                wide[pl.ds(at, part_cols), lev * LANES : (lev + 1) * LANES] = recvs[part][
                    tab[source_row * devices + lev * sections + q]
                ]
            return carry

        lax.fori_loop(0, sections, gather, 0)
        wide[:, 0:padded] = split_dot(wide[...], embed_ref[...])

        def divide(q, carry):
            denom = jnp.zeros((1, padded), jnp.float32)
            for lev in range(NLEV):
                denom = denom + cover_ref[lev : lev + 1, :] * tab[
                    3 * devices + lev * sections + q
                ].astype(jnp.float32)
            inverse = 1.0 / jnp.where(denom > 0.0, denom, 1.0)
            at = pl.multiple_of(q * part_cols, part_cols)
            value = wide[pl.ds(at, part_cols), 0:padded] * inverse
            wide[pl.ds(at, part_cols), 0:padded] = value
            if keep:
                kept[q, cols] = value
            return carry

        lax.fori_loop(0, sections, divide, 0)
        picked = split_dot(wide[:, 0:padded], take_ref[...])
        for lev in range(NLEV):
            packs[pl.ds(lev * sections, sections)] = picked[
                :, lev * LANES : (lev + 1) * LANES
            ].reshape(sections, part_cols, LANES)

        def answer(across, j):
            to = partner(across, j)
            send2[to, cols] = packs[tab[2 * devices + to]]
            copy_of(send2, out_ref, 1, part, across, j).start()

        each_partner(answer)
        out_ref[me, cols] = packs[tab[2 * devices + me]]

    if keep:
        for q in range(sections):
            keep_ref[:, q * section_rows : (q + 1) * section_rows] = kept[q, :, 0:section_rows]
    for part in range(parts):
        each_partner(lambda across, j: copy_of(send2, out_ref, 1, part, across, j).wait())


def local(start_field, col_speed, row_speed, levels, coeffs, assign_first, assign_second, owner_of):
    forward, backward, stacked, cover, section_rows, padded = row_tables()
    forward = jnp.asarray(forward, jnp.bfloat16)
    backward = jnp.asarray(backward, jnp.bfloat16)
    embed = jnp.asarray(stacked, jnp.bfloat16)
    take = jnp.asarray(stacked.T, jnp.bfloat16)
    cover = jnp.asarray(cover, jnp.float32)
    stencils = jnp.asarray(stencil_tables(), jnp.bfloat16)
    devices = lax.axis_size("grid")
    cells, lanes = start_field.shape[1:]
    block = cells // devices
    sections = devices // NLEV
    parts = 2 if block % 16 == 0 else 1
    columns = col_speed.reshape(1, cells)

    def stage(x, assign, assign_next, count, pre, post, in_map, out_map, tables):
        args = [levels, coeffs, assign, assign_next, owner_of, row_speed, x, columns, stencils]
        specs = [SMEM_SPEC] * 6 + [VMEM_SPEC] * 3
        if pre:
            args.append(backward)
            specs.append(VMEM_SPEC)
        if post:
            args.append(forward)
            specs.append(VMEM_SPEC)
        shape = (devices, block, lanes) if post else (1, cells, lanes)
        outs = [jax.ShapeDtypeStruct(shape, jnp.float32)]
        out_specs = [VMEM_SPEC]
        if tables:
            outs.append(jax.ShapeDtypeStruct((4 * devices,), jnp.int32))
            out_specs.append(SMEM_SPEC)
        return pl.pallas_call(
            functools.partial(local_kernel, count, pre, post, in_map, out_map, tables, devices),
            out_shape=outs,
            in_specs=specs,
            out_specs=out_specs,
            scratch_shapes=[
                pltpu.VMEM((2 * cells, lanes), jnp.float32),
                pltpu.VMEM((cells, lanes), jnp.float32),
            ],
        )(*args)

    def exchange(x, tab, source_row, keep, collective_id):
        outs = [jax.ShapeDtypeStruct((devices, block, lanes), jnp.float32)]
        if keep:
            outs.append(jax.ShapeDtypeStruct((block, sections * section_rows), jnp.float32))
        return pl.pallas_call(
            functools.partial(exchange_kernel, source_row, keep, devices, parts, section_rows),
            out_shape=outs,
            in_specs=[SMEM_SPEC] + [VMEM_SPEC] * 4,
            out_specs=[VMEM_SPEC] * len(outs),
            scratch_shapes=[
            ]
            + [pltpu.VMEM((devices, block // parts, lanes), jnp.float32)] * parts
            + [
                pltpu.VMEM((sections * block // parts, NLEV * lanes), jnp.float32),
                pltpu.VMEM((devices, block // parts, lanes), jnp.float32),
                pltpu.VMEM((devices, block, lanes), jnp.float32),
                pltpu.VMEM((sections, block, padded), jnp.float32),
                pltpu.SemaphoreType.DMA((4 * parts, devices)),
            ],
            compiler_params=pltpu.CompilerParams(
                collective_id=collective_id, has_side_effects=True
            ),
        )(tab, x, embed, take, cover)

    outgoing, tab = stage(
        start_field, assign_first, assign_second, STEPS, False, True, False, False, True
    )
    (restricted,) = exchange(outgoing, tab, 0, False, 0)
    (outgoing,) = stage(
        restricted, assign_second, assign_second, STEPS, True, True, False, True, False
    )
    restricted, combined = exchange(outgoing, tab, 1, True, 1)
    (final,) = stage(restricted, assign_second, assign_second, 1, True, False, True, False, False)
    return combined, final


def solution(mesh):
    placed = (
        P(("groups", "grid"), None, None),
        P(),
        P(),
        P("groups"),
        P("groups"),
        P("groups"),
        P("groups"),
        P("groups"),
    )
    return jax.shard_map(
        local,
        mesh=mesh,
        in_specs=placed,
        out_specs=(P(("groups", "grid"), None), P(("groups", "grid"), None, None)),
        check_vma=False,
    )
```
